32 devices in a mesh: look: 16 (over z, y, core), swath: 2 (over x).
Axes of the slice: x: 2, y: 2, z: 4, core: 2. Of those that a mesh axis runs over, the one named last changes fastest.
Arguments:
- images: bfloat16 [32, 8, 2, 512, 512], P('look', 'swath'), may hold values from -6 to 6
- patch_weight: float32 [8], P('swath'), may hold values from 1 to 10
- pair_mask: int32 [32, 4], P('look'), may hold values 0 or 1
Outputs:
- drift: float32 [32, 4, 256, 256], P('look', None, 'swath')
The draws below stay inside these ranges and needn't reach their ends.
All inputs are finite; a program needn't handle non-finite values. No bound on the sum of `pair_mask` on one device may be relied on, other than what follows from the above.
Results may differ from the reference program's by a relative error of at most 0.015.
Values may be sent and summed in bfloat16 or wider, within the bound.
A program may use at most 128 MiB of HBM per device.

```python
import math
import jax
import jax.numpy as jnp
from jax import lax

PIX = 512
BAND = 256
WIN = 256
LAGS = 4
LOOKS = 32
PATCHES = 8


def place_ends(drawn, own_key, smallest, largest):
    longest = drawn.shape.index(max(drawn.shape))
    spots = []
    for shift in (0, 1):
        where = [jax.random.randint(jax.random.fold_in(own_key, axis), (), 0, length) for axis, length in enumerate(drawn.shape)]
        where[longest] = (where[longest] + shift) % drawn.shape[longest]
        spots.append(tuple(where))
    return drawn.at[spots[0]].set(smallest).at[spots[1]].set(largest)


def level_of(own_key, extent, cuts, least, high):
    loudness, own = 1.0, jax.random.fold_in(own_key, 6)
    for axis_at, shards_of in cuts:
        steps = jnp.exp(jax.random.uniform(jax.random.fold_in(own, axis_at), (shards_of,), jnp.float32, least / len(cuts), high / len(cuts)))
        loudness = loudness * jnp.repeat(steps, extent[axis_at] // shards_of).reshape([-1 if axis == axis_at else 1 for axis in range(len(extent))])
    return loudness


def centred(key, shape, spread, limit, pieces=(), kind=jnp.bfloat16):
    factor_of = level_of(key, shape, pieces, -0.22, 0.18) if pieces else 1.0
    drawn = jax.random.normal(key, shape, jnp.float32) * spread * factor_of
    return jnp.minimum(jnp.maximum(drawn, -limit), limit).astype(kind)


def setup_inputs(seed: int = 0) -> dict:
    key_list = jax.random.split(jax.random.key(seed), 4)
    images = centred(key_list[0], (LOOKS, PATCHES, 2, PIX, PIX), 1.0, 6.0, ((0, 16), (1, 2)))
    patch_weight = jnp.clip(jnp.exp(math.log(10.0) - 2.3025851 * jax.random.uniform(key_list[1], (PATCHES,), jnp.float32) ** level_of(key_list[1], (PATCHES,), ((0, 2),), -0.2, 0.2)), 1.0, 10.0)
    pair_mask = place_ends((jax.random.randint(key_list[2], (LOOKS, LAGS), 0, 4) < 3).astype(jnp.int32), jax.random.fold_in(key_list[2], 1), 0, 1)
    return dict(images=images, patch_weight=patch_weight, pair_mask=pair_mask)


def tables(rows, cols, row_shift, col_shift, sign):
    row_ids = jnp.arange(rows, dtype=jnp.int32) - row_shift
    col_ids = jnp.arange(cols, dtype=jnp.int32) - col_shift
    phase = row_ids[:, None] * col_ids[None, :] % PIX
    angle = 2.0 * math.pi / PIX * phase.astype(jnp.float32)
    return (jnp.cos(angle).astype(jnp.bfloat16), (sign * jnp.sin(angle)).astype(jnp.bfloat16))

def fdot(form, left, right):
    return jnp.einsum(form, left.astype(jnp.float32), right.astype(jnp.float32))

def spectra(block, fwd_re, fwd_im):
    img_re = block[:, 0]
    img_im = block[:, 1]
    rows_re = (fdot('kn,anm->akm', fwd_re, img_re) - fdot('kn,anm->akm', fwd_im, img_im)).astype(jnp.bfloat16)
    rows_im = (fdot('kn,anm->akm', fwd_re, img_im) + fdot('kn,anm->akm', fwd_im, img_re)).astype(jnp.bfloat16)
    spec_re = (fdot('akm,lm->akl', rows_re, fwd_re) - fdot('akm,lm->akl', rows_im, fwd_im)).astype(jnp.bfloat16)
    spec_im = (fdot('akm,lm->akl', rows_re, fwd_im) + fdot('akm,lm->akl', rows_im, fwd_re)).astype(jnp.bfloat16)
    return jnp.stack([spec_re, spec_im], axis=1)

def surface_of(own, partner, weights, inv_re, inv_im):
    own_re = own[:, 0].astype(jnp.float32)
    own_im = own[:, 1].astype(jnp.float32)
    par_re = partner[:, 0].astype(jnp.float32)
    par_im = partner[:, 1].astype(jnp.float32)
    cross_re = (own_re * par_re + own_im * par_im).astype(jnp.bfloat16)
    cross_im = (own_im * par_re - own_re * par_im).astype(jnp.bfloat16)
    shift_re = (fdot('tf,pfg->ptg', inv_re, cross_re) - fdot('tf,pfg->ptg', inv_im, cross_im)).astype(jnp.bfloat16)
    shift_im = (fdot('tf,pfg->ptg', inv_re, cross_im) + fdot('tf,pfg->ptg', inv_im, cross_re)).astype(jnp.bfloat16)
    real_part = fdot('ptg,ug->ptu', shift_re, inv_re) - fdot('ptg,ug->ptu', shift_im, inv_im)
    return jnp.einsum('p,ptu->tu', weights, real_part)

def reference(images, patch_weight, pair_mask):
    fwd_re, fwd_im = tables(BAND, PIX, BAND // 2, 0, -1.0)
    inv_re, inv_im = tables(WIN, BAND, WIN // 2, BAND // 2, 1.0)
    spectrum = lax.map(lambda block: spectra(block, fwd_re, fwd_im), images)

    def energy_of(spec):
        sq = spec.astype(jnp.float32)
        return jnp.sum(patch_weight * lax.optimization_barrier(jnp.sum(sq * sq, axis=(1, 2, 3))))
    energy = lax.map(energy_of, spectrum)
    scale = BAND * math.sqrt(PATCHES)

    def one_look(look):
        own = lax.dynamic_index_in_dim(spectrum, look, 0, keepdims=False)
        outs = []
        for offset in (1, 2, 3, LOOKS // 2):
            mate = ((look + offset) % LOOKS).astype(jnp.int32)
            partner = lax.dynamic_index_in_dim(spectrum, mate, 0, keepdims=False)
            surf = surface_of(own, partner, patch_weight, inv_re, inv_im)
            denom = jnp.sqrt(energy[look] * energy[mate])
            outs.append(surf * scale / denom)
        return jnp.stack(outs, axis=0)
    surfaces = lax.map(one_look, jnp.arange(LOOKS, dtype=jnp.int32))
    return surfaces * pair_mask.astype(jnp.float32)[:, :, None, None]
```

```python
import functools
import math

import jax
import jax.numpy as jnp
import numpy as np
from jax import lax
from jax.experimental import pallas as pl
from jax.experimental.pallas import tpu as pltpu
from jax.sharding import PartitionSpec as P

PIX = 512
BAND = 256
WIN = 256
HALF = PIX // 2


def phases(rows, cols, row_shift, col_shift):
    phase = (rows[:, None] - row_shift) * (cols[None, :] - col_shift) % PIX
    angle = 2.0 * math.pi / PIX * phase
    return np.cos(angle), np.sin(angle)


def forward_tables():
    left, right = [], []
    for parity in (0, 1):
        re, im = phases(np.arange(parity, BAND, 2), np.arange(HALF), BAND // 2, 0)
        im = -im
        left.append(np.block([[re, -im], [im, re]]))
        right.append(np.block([[re.T, im.T], [-im.T, re.T]]))
    return jnp.asarray(np.stack(left), jnp.bfloat16), jnp.asarray(np.stack(right), jnp.bfloat16)


def inverse_tables():
    order = np.concatenate([np.arange(0, BAND, 2), np.arange(1, BAND, 2)])
    re, im = phases(np.arange(WIN), order, WIN // 2, BAND // 2)
    first = np.concatenate([re, im], axis=0)
    second = np.stack([re.T, im.T])
    return jnp.asarray(first, jnp.bfloat16), jnp.asarray(second, jnp.bfloat16)


def dot(left, right):
    return jnp.dot(left, right, preferred_element_type=jnp.float32)


ROWS = 32
MESH = pl.DeviceIdType.MESH


def spectrum_of(img, left_ref, right_ref):
    re0, re1 = img[0, :HALF, :], img[0, HALF:, :]
    im0, im1 = img[1, :HALF, :], img[1, HALF:, :]
    even = dot(left_ref[0], jnp.concatenate([re0 + re1, im0 + im1], axis=0))
    odd = dot(left_ref[1], jnp.concatenate([re0 - re1, im0 - im1], axis=0))
    quarter = BAND // 2
    parts = []
    for at in (0, quarter):
        parts.append(jnp.concatenate([even[at : at + quarter], odd[at : at + quarter]], axis=0))
    plus = [(part[:, :HALF] + part[:, HALF:]).astype(jnp.bfloat16) for part in parts]
    minus = [(part[:, :HALF] - part[:, HALF:]).astype(jnp.bfloat16) for part in parts]
    spec_even = dot(jnp.concatenate(plus, axis=1), right_ref[0]).astype(jnp.bfloat16)
    spec_odd = dot(jnp.concatenate(minus, axis=1), right_ref[1]).astype(jnp.bfloat16)
    return spec_even, spec_odd


def squares_of(spec_even, spec_odd):
    total = spec_even.astype(jnp.float32) ** 2 + spec_odd.astype(jnp.float32) ** 2
    folded = jnp.sum(total.reshape(BAND // 8, 8, BAND), axis=0)
    return folded[:, : BAND // 2] + folded[:, BAND // 2 :]


def cross_into(w_ref, a_ref, b_ref, cre, cim):
    patches = a_ref.shape[0]

    def step(i, carry):
        rows = pl.ds(pl.multiple_of(i * ROWS, ROWS), ROWS)
        re = jnp.zeros((ROWS, BAND), jnp.float32)
        im = jnp.zeros((ROWS, BAND), jnp.float32)
        for p in range(patches):
            weight = w_ref[p]
            ar = a_ref[p, 0, rows, :].astype(jnp.float32) * weight
            ai = a_ref[p, 1, rows, :].astype(jnp.float32) * weight
            br = b_ref[p, 0, rows, :].astype(jnp.float32)
            bi = b_ref[p, 1, rows, :].astype(jnp.float32)
            re += ar * br + ai * bi
            im += ai * br - ar * bi
        cre[rows, :] = re.astype(jnp.bfloat16)
        cim[rows, :] = im.astype(jnp.bfloat16)
        return carry

    lax.fori_loop(0, BAND // ROWS, step, 0)


def halves(first_ref, second_ref, cre, cim):
    from_re = dot(first_ref[...], cre[...]).astype(jnp.bfloat16)
    from_im = dot(first_ref[...], cim[...]).astype(jnp.bfloat16)
    keep = dot(from_re[:WIN], second_ref[0]) - dot(from_re[WIN:], second_ref[1])
    turn = dot(from_im[:WIN], second_ref[1]) + dot(from_im[WIN:], second_ref[0])
    return keep, turn


OWN, NEAR, FAR, OPP, LAST, HIGH, LOW = 0, 2, 4, 5, 7, 10, 13
BUFFERS = 16
OUTS = 8
HERE, ACROSS, LAST_EVEN, LAST_ODD, ZERO, ONE, HALF_EVEN, HALF_ODD = range(8)
TO_MATE, TO_LAST = 1, 2


def pair_step(a, b, out, to=HERE, wait_a=False, wait_b=False, back=None, relay=(0, 0), compute=True, late=False):
    back_to, back_out = back if back else (HERE, 0)
    fields = (
        (a, 16), (b, 16), (int(wait_a), 2), (int(wait_b), 2), (int(compute), 2), (int(back is not None), 2),
        (to, 8), (out, 8), (back_to, 8), (back_out, 8), (relay[0], 4), (relay[1], 16), (int(late), 2),
    )
    code = 0
    for value, base in reversed(fields):
        code = code * base + value
    return code


BASES = (16, 16, 2, 2, 2, 2, 8, 8, 8, 8, 4, 16, 2)


def decode(code):
    values = []
    for base in BASES:
        values.append(lax.rem(code, base))
        code = lax.div(code, base)
    return values


def relay_step(b, relay):
    return pair_step(0, b, 0, wait_b=True, relay=relay, compute=False)


def relay_unit(b, p, relay):
    return pair_step(p, b, 0, relay=relay, compute=False)


def opposite(k):
    return pair_step(OWN + k, OPP + k, 4 * k + 3, wait_b=True, back=(ACROSS, 4 * k + 3))


def step_lists():
    first = [pair_step(OWN, OWN + 1, 0)]
    near_pairs = [
        pair_step(OWN, NEAR, 1, wait_b=True),
        pair_step(OWN + 1, NEAR, 4),
        pair_step(OWN, NEAR + 1, 2, wait_b=True),
        pair_step(OWN + 1, NEAR + 1, 5),
    ]
    on_chip = first + near_pairs
    even = on_chip + [pair_step(OWN + 1, FAR, 6, wait_b=True)]
    to_far = (TO_MATE, FAR)

    def odd(end, late=False):
        return (
            first
            + [
                pair_step(OWN, NEAR, 1, wait_b=True, relay=to_far),
                pair_step(OWN + 1, NEAR, 4),
                pair_step(OWN + 1, FAR, 6, wait_b=True),
                pair_step(OWN, NEAR + 1, 2, wait_b=True, late=late),
                pair_step(OWN + 1, NEAR + 1, 5),
            ]
            + end
        )

    def pass_on(p, which):
        at = (NEAR, NEAR + 1, FAR)[which]
        return relay_unit(LOW + which, p, (TO_LAST, at))

    hub = (
        first
        + near_pairs[:1]
        + [pass_on(0, 0), pass_on(0, 2)]
        + near_pairs[1:]
        + [pass_on(p, which) for p in (1, 2, 3) for which in (0, 2)]
        + [
            pair_step(LAST, HIGH, 6, LAST_EVEN, wait_a=True, wait_b=True),
            pair_step(LOW, HIGH, 3, ZERO, back=(HALF_EVEN, 3)),
            pass_on(0, 1),
            pair_step(LAST + 2, HIGH, 4, LAST_ODD, wait_a=True),
            pair_step(LOW + 2, HIGH + 2, 3, ONE, wait_b=True, back=(HALF_ODD, 3)),
            pass_on(1, 1),
            pair_step(LAST + 2, HIGH + 2, 6, LAST_ODD),
            pass_on(2, 1),
            pass_on(3, 1),
            pair_step(LOW + 1, HIGH + 1, 7, ZERO, wait_b=True, back=(HALF_EVEN, 7)),
            pair_step(LAST + 2, HIGH + 1, 5, LAST_ODD),
            pair_step(LAST + 1, HIGH, 1, LAST_ODD, wait_a=True),
            pair_step(LAST + 1, HIGH + 1, 2, LAST_ODD),
            pair_step(OWN + 1, FAR, 6, wait_b=True),
        ]
    )
    hub_odd = first + [
        pair_step(OWN, NEAR + 1, 2, wait_b=True, relay=(TO_MATE, LAST)),
        pair_step(OWN + 1, NEAR + 1, 5),
        relay_step(NEAR, to_far),
        relay_step(FAR, (TO_MATE, LAST + 1)),
        opposite(1),
        pair_step(OWN, NEAR, 1),
        pair_step(OWN + 1, NEAR, 4),
        pair_step(OWN + 1, FAR, 6),
    ]
    last_even = on_chip + [
        opposite(1),
        pair_step(OPP + 1, FAR, 6, ACROSS, wait_b=True),
    ]
    last_odd = first + [
        relay_step(NEAR, to_far),
        opposite(0),
        pair_step(OPP, NEAR, 1, ACROSS),
        opposite(1),
        pair_step(OPP + 1, NEAR, 4, ACROSS),
        pair_step(OPP + 1, FAR, 6, ACROSS, wait_b=True),
        pair_step(OPP, NEAR + 1, 2, ACROSS, wait_b=True),
        pair_step(OPP + 1, NEAR + 1, 5, ACROSS),
    ]
    return (
        even,
        odd([], late=True),
        even,
        odd([opposite(1)]),
        hub,
        hub_odd,
        last_even,
        last_odd,
        even,
        odd([opposite(1)]),
        even + [opposite(0), opposite(1)],
        odd([opposite(0)], late=True),
        on_chip + [opposite(0)],
        first,
    )


BACK = ((3, 7), (3, 7), (3, 7), (3,), (3, 7), (3,), (3, 6), (1, 2, 4, 5, 6), (3, 7), (3,), (), (7,), (6, 7), (1, 2, 3, 4, 5, 6, 7))
SENT = ((), (1,), (0, 1), (0,), (0, 1), (0,), (0,), (), (), (), (), (1,), (1,), (0, 1))
LEAD = (0, 0, 0, 0, 0, 0, 1, 1, 0, 0, 0, 0, 0, 0)
LATE = (1, 11)
STEPS = max(len(steps) for steps in step_lists())


def pick(index, values):
    result = jnp.int32(values[0]) if isinstance(values[0], int) else values[0]
    for at, value in enumerate(values[1:], 1):
        result = jnp.where(index == at, value, result)
    return result


def bit(mask, at):
    return lax.rem(lax.div(mask, jnp.int32(2**at)), 2) == 1


def kernel(nlook, nswath, w_ref, mask_ref, img_ref, left_hbm, right_hbm, first_hbm, second_hbm, out_ref, factor_ref,
           left_ref, right_ref, first_ref, second_ref, img, spec, energy, heard, cre, cim, surf, outbox, inbox, turned, backbox,
           table_sem, img_sem, near_send, far_send, opp_send, relay_send, spec_recv,
           heard_send, heard_recv, box_send, box_recv, back_send, back_recv):
    looks, patches = img_ref.shape[:2]
    half = nlook // 2
    hub = half - 4
    me, lane = lax.axis_index("look"), lax.axis_index("swath")
    chip, odd = lax.div(me, 2), lax.rem(me, 2)
    low = me < half
    place = jnp.where(low, jnp.int32(1), jnp.int32(5))
    for at, value in ((0, 0), (half // 2 - 2, 2), (half // 2 - 1, 3), (half // 2, 4), (half - 1, 6)):
        place = jnp.where(chip == at, value, place)
    role = 2 * place + odd
    lists = step_lists()
    count = pick(role, [len(steps) for steps in lists])
    codes = [pick(role, [steps[i] if i < len(steps) else 0 for steps in lists]) for i in range(STEPS)]
    backs = pick(role, [sum(2**at for at in outs) for outs in BACK])
    sents = pick(role, [sum(2**at for at in ks) for ks in SENT])
    lead = pick(role, list(LEAD))
    late = functools.reduce(jnp.logical_or, [role == at for at in LATE])

    def device(look_by, swath_by=0):
        return (lax.rem(me + look_by + nlook, nlook), lax.rem(lane + swath_by, nswath))

    def look_at(u):
        return lax.rem(lead + u // patches, looks)

    def load(u):
        return pltpu.make_async_copy(img_ref.at[look_at(u), u % patches], img.at[u], img_sem.at[u])

    tables = [
        pltpu.make_async_copy(src, dst, table_sem.at[i])
        for i, (src, dst) in enumerate(
            ((left_hbm, left_ref), (right_hbm, right_ref), (first_hbm, first_ref), (second_hbm, second_ref))
        )
    ]
    load(0).start()
    tables[0].start()
    tables[1].start()
    for u in range(1, looks * patches):
        load(u).start()
    tables[2].start()
    tables[3].start()

    barrier = pltpu.get_barrier_semaphore()
    greeted = 0
    for look_by in (0, 1, -1, 2, -2, half):
        for by in range(nswath):
            if look_by or by:
                greeted += 1
                pl.semaphore_signal(barrier, inc=1, device_id=device(look_by, by), device_id_type=MESH)
    met = (0, 1, half - 1, half, half + 1)
    meets = functools.reduce(jnp.logical_or, [me == at for at in met])

    @pl.when(me == hub)
    def _():
        for at in met:
            pl.semaphore_signal(barrier, inc=1, device_id=(jnp.int32(at), lane), device_id_type=MESH)

    @pl.when(meets)
    def _():
        pl.semaphore_signal(barrier, inc=1, device_id=(jnp.int32(hub), lane), device_id_type=MESH)

    expected = jnp.where(me == hub, greeted + len(met), jnp.where(meets, greeted + 1, greeted))

    def remote(src, dst, send, recv, to):
        return pltpu.make_async_remote_copy(
            src_ref=src, dst_ref=dst, send_sem=send, recv_sem=recv, device_id=to, device_id_type=MESH
        )

    def arrival(at, p):
        return remote(spec.at[at, p], spec.at[at, p], relay_send.at[at, p], spec_recv.at[at, p], device(-1))

    def to_near(look, p):
        meeting = jnp.logical_or(me == 0, me == half)
        to = jnp.where(meeting, hub, lax.rem(me - 1 + nlook, nlook))
        at = jnp.where(me == 0, LOW, jnp.where(me == half, HIGH, NEAR)) + look
        return remote(spec.at[OWN + look, p], spec.at[at, p], near_send.at[look, p], spec_recv.at[at, p], (to, lane))

    def to_far(look, p):
        meeting = jnp.logical_or(look == 1, jnp.logical_or(me == 1, me == half + 1))
        to = jnp.where(meeting, hub, lax.rem(me - 2 + nlook, nlook))
        at = jnp.where(me == 1, LOW + 2, jnp.where(me == half + 1, HIGH + 2, FAR))
        at = jnp.where(look == 1, LAST + 2, at)
        return remote(spec.at[OWN + look, p], spec.at[at, p], far_send.at[look, p], spec_recv.at[at, p], (to, lane))

    def to_opp(look, p):
        at = OPP + look
        return remote(spec.at[OWN + look, p], spec.at[at, p], opp_send.at[look, p], spec_recv.at[at, p], device(half))

    def relayed(b, p, mate, at):
        to = jnp.where(mate, lax.rem(me - 1 + nlook, nlook), half - 1)
        return remote(spec.at[b, p], spec.at[at, p], relay_send.at[b, p], spec_recv.at[at, p], (to, lane))

    def each_send(look, p, act, all_opp=False):
        has_far = jnp.logical_and(odd == 1, jnp.logical_or(look == 0, me == half - 1))
        has_opp = jnp.where(look == 0, bit(sents, 0), bit(sents, 1))

        @pl.when(has_opp if all_opp else jnp.logical_and(has_opp, jnp.logical_not(late)))
        def _():
            act(to_opp(look, p))

        act(to_near(look, p))

        @pl.when(has_far)
        def _():
            act(to_far(look, p))

    for look in range(looks):
        energy[look] = jnp.zeros((8, 128), jnp.float32)

    def forward(u, carry):
        @pl.when(u == 1)
        def _():
            pl.semaphore_wait(barrier, expected)

        @pl.when(u > 0)
        def _():
            each_send(look_at(u - 1), (u - 1) % patches, lambda copy: copy.start())

        look, p = look_at(u), u % patches
        load(u).wait()
        spec_even, spec_odd = spectrum_of(img.at[u], left_ref, right_ref)
        quarter = BAND // 2
        spec[OWN + look, p, 0, :, :quarter] = spec_even[:, :quarter]
        spec[OWN + look, p, 0, :, quarter:] = spec_odd[:, :quarter]
        spec[OWN + look, p, 1, :, :quarter] = spec_even[:, quarter:]
        spec[OWN + look, p, 1, :, quarter:] = spec_odd[:, quarter:]
        energy[look] += w_ref[p] * squares_of(spec_even, spec_odd)
        return carry

    tables[0].wait()
    tables[1].wait()
    units = looks * patches
    lax.fori_loop(0, units, forward, 0)
    each_send(look_at(units - 1), (units - 1) % patches, lambda copy: copy.start())

    tell = []
    for d, look_by in enumerate((0, 1, 2, half)):
        for by in range(nswath):
            if look_by or by:
                tell.append(remote(energy, heard.at[d, by], heard_send.at[d, by], heard_recv.at[d, by],
                                   device(-look_by, by)))
    for copy in tell:
        copy.start()

    rows = WIN // nswath
    mine = pl.ds(pl.multiple_of(lane * rows, rows), rows)

    def outgoing(slot, by):
        at = pl.ds(pl.multiple_of(lax.rem(lane + by, nswath) * rows, rows), rows)
        return remote(outbox.at[slot, at], inbox.at[by - 1, slot], box_send.at[by - 1, slot],
                      box_recv.at[by - 1, slot], device(0, by))

    def returned(slot, to, out):
        where = pick(to, [me, lax.rem(me + half, nlook), half - 2, half - 1, 0, 1, half, half + 1])
        return remote(turned.at[slot], backbox.at[out], back_send.at[slot], back_recv.at[out], (where, lane))

    def finish(i, slot, to, out):
        value = surf[slot // STEPS * 2 + i % 2, mine, :]
        for by in range(1, nswath):
            outgoing(slot, by).wait_recv()
            value = value + inbox[by - 1, slot].astype(jnp.float32)

        @pl.when(to == HERE)
        def _():
            out_ref[out] = value

        @pl.when(to != HERE)
        def _():
            turned[slot] = value.astype(jnp.bfloat16)
            returned(slot, to, out).start()

    def code_at(i):
        return pick(i, codes)

    tables[2].wait()
    tables[3].wait()

    def step(i, carry):
        a, b, wait_a, wait_b, compute, back, _, _, _, _, relay, relay_at, now = decode(code_at(i))

        @pl.when(jnp.logical_and(compute == 0, wait_b == 0))
        def _():
            arrival(b, a).wait_recv()
            relayed(b, a, relay == TO_MATE, relay_at).start()

        @pl.when(wait_a == 1)
        def _():
            for p in range(patches):
                arrival(a, p).wait_recv()

        @pl.when(wait_b == 1)
        def _():
            for p in range(patches):
                arrival(b, p).wait_recv()

                @pl.when(relay != 0)
                def _():
                    relayed(b, p, relay == TO_MATE, relay_at).start()

        @pl.when(now == 1)
        def _():
            for p in range(patches):
                to_opp(1, p).start()

        @pl.when(compute == 1)
        def _():
            cross_into(w_ref, spec.at[a], spec.at[b], cre, cim)
            keep, turn = halves(first_ref, second_ref, cre, cim)
            value = keep - turn
            surf[i % 2] = value
            outbox[i] = value.astype(jnp.bfloat16)
            value = keep + turn
            surf[2 + i % 2] = value
            outbox[STEPS + i] = value.astype(jnp.bfloat16)
            for by in range(1, nswath):
                outgoing(i, by).start()

            @pl.when(back == 1)
            def _():
                for by in range(1, nswath):
                    outgoing(STEPS + i, by).start()

        @pl.when(i > 0)
        def _():
            settle(i - 1)

        return carry

    def settle(i):
        _, _, _, _, compute, back, to, out, back_to, back_out, _, _, _ = decode(code_at(i))

        @pl.when(compute == 1)
        def _():
            @pl.when(back == 1)
            def _():
                finish(i, STEPS + i, back_to, back_out)

            finish(i, i, to, out)

    lax.fori_loop(0, count, step, 0)
    settle(count - 1)

    for copy in tell:
        copy.wait_recv()
    total = []
    for d in range(4):
        for look in range(looks):
            parts = energy[look] if d == 0 else heard[d, 0, look]
            for by in range(1, nswath):
                parts = parts + heard[d, by, look]
            total.append(jnp.sum(parts, axis=(0, 1), keepdims=True))
    scale = BAND * math.sqrt(patches * nswath)

    def factor(look, lag):
        mate = total[look + lag + 1] if lag < 3 else total[3 * looks + look]
        return mask_ref[look, lag].astype(jnp.float32) * scale / jnp.sqrt(total[look] * mate)

    for look in range(looks):
        for lag in range(4):
            factor_ref[look, lag : lag + 1, :] = jnp.broadcast_to(factor(look, lag), (1, WIN))

    def fetch(out, carry):
        @pl.when(bit_of(backs, out))
        def _():
            remote(turned.at[0], backbox.at[out], back_send.at[0], back_recv.at[out], device(half)).wait_recv()
            out_ref[out] = backbox[out].astype(jnp.float32)

        return carry

    def bit_of(mask, at):
        return pick(at, [lax.rem(lax.div(mask, jnp.int32(2**k)), 2) for k in range(OUTS)]) == 1

    lax.fori_loop(0, OUTS, fetch, 0)

    def drain_sends(u, carry):
        each_send(u // patches, u % patches, lambda copy: copy.wait_send(), True)
        return carry

    lax.fori_loop(0, units, drain_sends, 0)

    def drain_steps(i, carry):
        a, b, _, wait_b, compute, back, to, out, back_to, back_out, relay, relay_at, _ = decode(code_at(i))

        @pl.when(jnp.logical_and(relay != 0, wait_b == 1))
        def _():
            for p in range(patches):
                relayed(b, p, relay == TO_MATE, relay_at).wait_send()

        @pl.when(jnp.logical_and(compute == 0, wait_b == 0))
        def _():
            relayed(b, a, relay == TO_MATE, relay_at).wait_send()

        @pl.when(compute == 1)
        def _():
            for by in range(1, nswath):
                outgoing(i, by).wait_send()

            @pl.when(to != HERE)
            def _():
                returned(i, to, out).wait_send()

            @pl.when(back == 1)
            def _():
                for by in range(1, nswath):
                    outgoing(STEPS + i, by).wait_send()
                returned(STEPS + i, back_to, back_out).wait_send()

        return carry

    lax.fori_loop(0, count, drain_steps, 0)
    for copy in tell:
        copy.wait_send()


def per_device(images, patch_weight, pair_mask):
    nlook = lax.axis_size("look")
    nswath = lax.axis_size("swath")
    looks, patches = images.shape[:2]
    left, right = forward_tables()
    first, second = inverse_tables()
    rows = WIN // nswath
    vmem = pl.BlockSpec(memory_space=pltpu.VMEM)
    smem = pl.BlockSpec(memory_space=pltpu.SMEM)
    dma = pltpu.SemaphoreType.DMA
    unit = (2, BAND, BAND)
    others = max(nswath - 1, 1)
    surfaces, factors = pl.pallas_call(
        functools.partial(kernel, nlook, nswath),
        in_specs=[smem, smem] + [pl.BlockSpec(memory_space=pltpu.HBM)] * 5,
        out_specs=[vmem, vmem],
        out_shape=[
            jax.ShapeDtypeStruct((OUTS, rows, WIN), jnp.float32),
            jax.ShapeDtypeStruct((looks, 4, WIN), jnp.float32),
        ],
        scratch_shapes=[
            pltpu.VMEM(left.shape, jnp.bfloat16),
            pltpu.VMEM(right.shape, jnp.bfloat16),
            pltpu.VMEM(first.shape, jnp.bfloat16),
            pltpu.VMEM(second.shape, jnp.bfloat16),
            pltpu.VMEM((looks * patches, 2, PIX, PIX), jnp.bfloat16),
            pltpu.VMEM((BUFFERS, patches) + unit, jnp.bfloat16),
            pltpu.VMEM((looks, 8, 128), jnp.float32),
            pltpu.VMEM((4, nswath, looks, 8, 128), jnp.float32),
            pltpu.VMEM((BAND, BAND), jnp.bfloat16),
            pltpu.VMEM((BAND, BAND), jnp.bfloat16),
            pltpu.VMEM((4, WIN, WIN), jnp.float32),
            pltpu.VMEM((2 * STEPS, WIN, WIN), jnp.bfloat16),
            pltpu.VMEM((others, 2 * STEPS, rows, WIN), jnp.bfloat16),
            pltpu.VMEM((2 * STEPS, rows, WIN), jnp.bfloat16),
            pltpu.VMEM((OUTS, rows, WIN), jnp.bfloat16),
            dma((4,)),
            dma((looks * patches,)),
            dma((looks, patches)),
            dma((looks, patches)),
            dma((looks, patches)),
            dma((BUFFERS, patches)),
            dma((BUFFERS, patches)),
            dma((4, nswath)),
            dma((4, nswath)),
            dma((others, 2 * STEPS)),
            dma((others, 2 * STEPS)),
            dma((2 * STEPS,)),
            dma((OUTS,)),
        ],
        compiler_params=pltpu.CompilerParams(
            collective_id=0, has_side_effects=True, vmem_limit_bytes=67043328
        ),
        name="autofocus",
    )(patch_weight, pair_mask, images, left, right, first, second)
    return surfaces.reshape(looks, 4, rows, WIN) * factors[:, :, None, :]


def solution(mesh):
    return jax.shard_map(
        per_device,
        mesh=mesh,
        in_specs=(P("look", "swath", None, None, None), P("swath"), P("look", None)),
        out_specs=P("look", None, "swath", None),
        check_vma=False,
    )
```

```python
import functools
import math

import jax
import jax.numpy as jnp
import numpy as np
from jax import lax
from jax.experimental import pallas as pl
from jax.experimental.pallas import tpu as pltpu
from jax.sharding import PartitionSpec as P

PIX = 512
BAND = 256
WIN = 256
HALF = PIX // 2


def phases(rows, cols, row_shift, col_shift):
    phase = (rows[:, None] - row_shift) * (cols[None, :] - col_shift) % PIX
    angle = 2.0 * math.pi / PIX * phase
    return np.cos(angle), np.sin(angle)


def forward_tables():
    left, right = [], []
    for parity in (0, 1):
        re, im = phases(np.arange(parity, BAND, 2), np.arange(HALF), BAND // 2, 0)
        im = -im
        left.append(np.block([[re, -im], [im, re]]))
        right.append(np.block([[re.T, im.T], [-im.T, re.T]]))
    return jnp.asarray(np.stack(left), jnp.bfloat16), jnp.asarray(np.stack(right), jnp.bfloat16)


def inverse_tables():
    order = np.concatenate([np.arange(0, BAND, 2), np.arange(1, BAND, 2)])
    re, im = phases(np.arange(WIN), order, WIN // 2, BAND // 2)
    first = np.concatenate([re, im], axis=0)
    second = np.stack([re.T, im.T])
    return jnp.asarray(first, jnp.bfloat16), jnp.asarray(second, jnp.bfloat16)


def dot(left, right):
    return jnp.dot(left, right, preferred_element_type=jnp.float32)


ROWS = 32
MESH = pl.DeviceIdType.MESH


def spectrum_of(img, left_ref, right_ref):
    re0, re1 = img[0, :HALF, :], img[0, HALF:, :]
    im0, im1 = img[1, :HALF, :], img[1, HALF:, :]
    even = dot(left_ref[0], jnp.concatenate([re0 + re1, im0 + im1], axis=0))
    odd = dot(left_ref[1], jnp.concatenate([re0 - re1, im0 - im1], axis=0))
    quarter = BAND // 2
    parts = []
    for at in (0, quarter):
        parts.append(jnp.concatenate([even[at : at + quarter], odd[at : at + quarter]], axis=0))
    plus = [(part[:, :HALF] + part[:, HALF:]).astype(jnp.bfloat16) for part in parts]
    minus = [(part[:, :HALF] - part[:, HALF:]).astype(jnp.bfloat16) for part in parts]
    spec_even = dot(jnp.concatenate(plus, axis=1), right_ref[0]).astype(jnp.bfloat16)
    spec_odd = dot(jnp.concatenate(minus, axis=1), right_ref[1]).astype(jnp.bfloat16)
    return spec_even, spec_odd


def squares_of(spec_even, spec_odd):
    total = spec_even.astype(jnp.float32) ** 2 + spec_odd.astype(jnp.float32) ** 2
    folded = jnp.sum(total.reshape(BAND // 8, 8, BAND), axis=0)
    return folded[:, : BAND // 2] + folded[:, BAND // 2 :]


def cross_into(w_ref, a_ref, b_ref, cre, cim):
    patches = a_ref.shape[0]

    def step(i, carry):
        rows = pl.ds(pl.multiple_of(i * ROWS, ROWS), ROWS)
        re = jnp.zeros((ROWS, BAND), jnp.float32)
        im = jnp.zeros((ROWS, BAND), jnp.float32)
        for p in range(patches):
            weight = w_ref[p]
            ar = a_ref[p, 0, rows, :].astype(jnp.float32) * weight
            ai = a_ref[p, 1, rows, :].astype(jnp.float32) * weight
            br = b_ref[p, 0, rows, :].astype(jnp.float32)
            bi = b_ref[p, 1, rows, :].astype(jnp.float32)
            re += ar * br + ai * bi
            im += ai * br - ar * bi
        cre[rows, :] = re.astype(jnp.bfloat16)
        cim[rows, :] = im.astype(jnp.bfloat16)
        return carry

    lax.fori_loop(0, BAND // ROWS, step, 0)


def halves(first_ref, second_ref, cre, cim):
    from_re = dot(first_ref[...], cre[...]).astype(jnp.bfloat16)
    from_im = dot(first_ref[...], cim[...]).astype(jnp.bfloat16)
    keep = dot(from_re[:WIN], second_ref[0]) - dot(from_re[WIN:], second_ref[1])
    turn = dot(from_im[:WIN], second_ref[1]) + dot(from_im[WIN:], second_ref[0])
    return keep, turn


OWN, NEAR, FAR, LOW, OPP, LAST, HIGH = 0, 2, 4, 5, 8, 10, 13
BUFFERS = 16
WHOLE = OPP
OUTS = 8
HERE, ACROSS, LAST_EVEN, LAST_ODD, ZERO, ONE, HALF_EVEN, HALF_ODD = range(8)
TO_MATE, TO_LAST = 1, 2


def pair_step(a, b, out, to=HERE, wait_a=False, wait_b=False, back=None, relay=(0, 0), compute=True, late=False,
              flush=False, direct=False):
    back_to, back_out = back if back else (HERE, 0)
    do = (a, b, int(wait_a), int(wait_b), int(compute), int(back is not None), relay[0], relay[1], int(late),
          int(flush), int(direct))
    end = (int(compute), int(back is not None and not direct), to, out, back_to, back_out)
    return do, end


DO_BASES = (16, 16, 2, 2, 2, 2, 4, 16, 2, 2, 2, 32)
END_BASES = (2, 2, 8, 8, 8, 8, 32)


def encode(values, bases):
    code = 0
    for value, base in zip(reversed(values), reversed(bases), strict=True):
        code = code * base + value
    return code


def decode(code, bases):
    values = []
    for base in bases:
        values.append(lax.rem(code, base))
        code = lax.div(code, base)
    return values


def coded(steps):
    codes, slot = [], 0
    for do, end in steps:
        codes.append((encode(do + (slot,), DO_BASES), encode(end + (slot,), END_BASES)))
        slot += do[4] + do[5]
    return codes


def relay_step(b, relay):
    return pair_step(0, b, 0, wait_b=True, relay=relay, compute=False)


def relay_unit(b, p, relay):
    return pair_step(p, b, 0, relay=relay, compute=False)


def opposite(k, direct=False, flush=False):
    out = 4 * k + 3
    return pair_step(OWN + k, OPP + k, out, wait_b=True, back=(ACROSS, out), direct=direct, flush=flush)


def step_lists():
    first = [pair_step(OWN, OWN + 1, 0)]
    near_pairs = [
        pair_step(OWN, NEAR, 1, wait_b=True),
        pair_step(OWN + 1, NEAR, 4),
        pair_step(OWN, NEAR + 1, 2, wait_b=True),
        pair_step(OWN + 1, NEAR + 1, 5),
    ]
    on_chip = first + near_pairs
    even = on_chip + [pair_step(OWN + 1, FAR, 6, wait_b=True)]
    to_far = (TO_MATE, FAR)

    def odd(end, late=False):
        return (
            first
            + [
                pair_step(OWN, NEAR, 1, wait_b=True, relay=to_far),
                pair_step(OWN + 1, NEAR, 4),
                pair_step(OWN + 1, FAR, 6, wait_b=True),
                pair_step(OWN, NEAR + 1, 2, wait_b=True, late=late),
                pair_step(OWN + 1, NEAR + 1, 5),
            ]
            + end
        )

    def pass_on(p, which):
        at = (NEAR, NEAR + 1, FAR)[which]
        return relay_unit(LOW + which, p, (TO_LAST, at))

    def pass_both(p):
        return [pass_on(p, 0), pass_on(p, 2)]

    hub = (
        pass_both(0)
        + first
        + near_pairs[:2]
        + pass_both(1)
        + near_pairs[2:]
        + pass_both(2)
        + pass_both(3)
        + [
            pair_step(LOW, HIGH, 3, ZERO, wait_b=True, back=(HALF_EVEN, 3)),
            pass_on(0, 1),
            pair_step(LOW + 2, HIGH + 2, 3, ONE, wait_b=True, back=(HALF_ODD, 3)),
            pass_on(1, 1),
            pass_on(2, 1),
            pair_step(LAST, HIGH, 6, LAST_EVEN, wait_a=True),
            pass_on(3, 1),
            pair_step(LAST + 2, HIGH, 4, LAST_ODD, wait_a=True),
            pair_step(LAST + 2, HIGH + 2, 6, LAST_ODD),
            pair_step(LAST + 1, HIGH, 1, LAST_ODD, wait_a=True),
            pair_step(LAST + 1, HIGH + 1, 2, LAST_ODD, wait_b=True),
            pair_step(LAST + 2, HIGH + 1, 5, LAST_ODD),
            pair_step(LOW + 1, HIGH + 1, 7, ZERO, back=(HALF_EVEN, 7)),
            pair_step(OWN + 1, FAR, 6, wait_b=True, flush=True),
        ]
    )
    hub_odd = first + [
        pair_step(OWN, NEAR + 1, 2, wait_b=True, relay=(TO_MATE, LAST)),
        pair_step(OWN + 1, NEAR + 1, 5),
        pair_step(OWN + 1, FAR, 6, wait_b=True, relay=(TO_MATE, LAST + 1)),
        relay_step(NEAR, to_far),
        opposite(1, True),
        pair_step(OWN, NEAR, 1),
        pair_step(OWN + 1, NEAR, 4),
    ]
    last_even = on_chip + [
        opposite(1),
        pair_step(0, FAR, 0, wait_b=True, compute=False, late=True),
        pair_step(OPP + 1, FAR, 6, ACROSS),
    ]
    last_odd = first + [
        relay_step(NEAR, to_far),
        opposite(0),
        pair_step(OPP, NEAR, 1, ACROSS),
        opposite(1),
        pair_step(OPP + 1, NEAR, 4, ACROSS),
        pair_step(OPP + 1, FAR, 6, ACROSS, wait_b=True),
        pair_step(OPP, NEAR + 1, 2, ACROSS, wait_b=True, flush=True),
        pair_step(OPP + 1, NEAR + 1, 5, ACROSS),
    ]
    return (
        even,
        odd([], late=True),
        even,
        odd([opposite(1, True)]),
        hub,
        hub_odd,
        last_even,
        last_odd,
        even,
        odd([opposite(1, True)]),
        even + [opposite(0), opposite(1, True, True)],
        odd([opposite(0)], late=True),
        on_chip + [opposite(0, True)],
        first,
    )


BACK = ((3, 7), (3,), (3,), (3,), (3,), (3,), (6,), (1, 2, 4, 5, 6), (3, 7), (3,), (), (), (6, 7), (1, 2, 3, 4, 5, 6, 7))
PARTS_OF = {1: 7, 2: 7, 4: 7, 6: 3, 11: 7}
PARTS_BY = (3, 5, 9, 10, 12)
HELD_BACK, FREES = {7: 2, 10: 1}, (6, 11)
SENT = ((), (1,), (0, 1), (0,), (0, 1), (0,), (0,), (), (), (), (), (1,), (1,), (0, 1))
LATE, LATE_NEAR = (1, 11), 6
AHEAD = 2
LAG = 2
HELD = 4
STEPS = max(len(steps) for steps in step_lists())
RESULTS = [sum(end[0] + end[1] for _, end in steps) for steps in step_lists()]
RETURNS = [sum(int(end[2] != HERE) + end[1] for _, end in steps) for steps in step_lists()]
SLOTS = max(sum(do[4] + do[5] for do, _ in steps) for steps in step_lists())


def looks_sent(role, patches):
    relayed = sum((patches if do[3] else 1) for do, _ in step_lists()[role] if do[6])
    return 2 + role % 2 + int(role == 7) + len(SENT[role]) + relayed // patches


def pick(index, values):
    result = jnp.int32(values[0]) if isinstance(values[0], int) else values[0]
    for at, value in enumerate(values[1:], 1):
        result = jnp.where(index == at, value, result)
    return result


def bit(mask, at):
    return lax.rem(lax.div(mask, jnp.int32(2**at)), 2) == 1


def kernel(nlook, nswath, w_ref, mask_ref, img_ref, left_hbm, right_hbm, first_hbm, second_hbm, out_hbm, factor_hbm,
           left_ref, right_ref, first_ref, second_ref, img, spec, energy, heard, cre, cim, surf, outbox, inbox, turned, backbox, parts, final, factors,
           table_sem, img_sem, unit_send, spec_recv,
           heard_send, heard_recv, box_send, box_recv, back_send, back_recv, parts_send, parts_recv, out_sem, ready, go):
    looks, patches = img_ref.shape[:2]
    half = nlook // 2
    hub = half - 4
    me, lane = lax.axis_index("look"), lax.axis_index("swath")
    chip, odd = lax.div(me, 2), lax.rem(me, 2)
    lead = jnp.where(chip == half // 2 - 1, 1, 0)

    def device(look_by, swath_by=0):
        return (lax.rem(me + look_by + nlook, nlook), lax.rem(lane + swath_by, nswath))

    def look_at(u):
        return lax.rem(lead + u // patches, looks)

    def load(u):
        return pltpu.make_async_copy(img_ref.at[look_at(u), u % patches], img.at[u], img_sem.at[u % AHEAD])

    tables = [
        pltpu.make_async_copy(src, dst, table_sem.at[i])
        for i, (src, dst) in enumerate(
            ((left_hbm, left_ref), (right_hbm, right_ref), (first_hbm, first_ref), (second_hbm, second_ref))
        )
    ]
    units = looks * patches
    load(0).start()
    tables[0].start()
    tables[1].start()
    for u in range(1, AHEAD):
        load(u).start()

    barrier = pltpu.get_barrier_semaphore()
    greeted = 0
    behind = []
    for look_by in (0, 1, -1, 2, -2, half):
        for by in range(nswath):
            if look_by or by:
                greeted += 1
                to = device(look_by, by)
                if look_by in (1, 2, half):
                    later = jnp.logical_and(to[0] < 2, me >= half)
                    behind.append((later, to))

                    @pl.when(jnp.logical_not(later))
                    def _():
                        pl.semaphore_signal(barrier, inc=1, device_id=to, device_id_type=MESH)
                else:
                    pl.semaphore_signal(barrier, inc=1, device_id=to, device_id_type=MESH)
    met = (0, 1, half - 1, half, half + 1)
    meets = functools.reduce(jnp.logical_or, [me == at for at in met])

    @pl.when(me == hub)
    def _():
        for at in met:
            pl.semaphore_signal(barrier, inc=1, device_id=(jnp.int32(at), lane), device_id_type=MESH)

    @pl.when(meets)
    def _():
        pl.semaphore_signal(barrier, inc=1, device_id=(jnp.int32(hub), lane), device_id_type=MESH)

    expected = jnp.where(me == hub, greeted + len(met), jnp.where(meets, greeted + 1, greeted))
    missing = jnp.where(me == 0, 3 * nswath, jnp.where(me == 1, 2 * nswath, 0))

    place = jnp.where(me < half, jnp.int32(1), jnp.int32(5))
    for at, value in ((0, 0), (half // 2 - 2, 2), (half // 2 - 1, 3), (half // 2, 4), (half - 1, 6)):
        place = jnp.where(chip == at, value, place)
    role = 2 * place + odd
    sents = pick(role, [sum(2**at for at in ks) for ks in SENT])
    late = functools.reduce(jnp.logical_or, [role == at for at in LATE])
    held_back = functools.reduce(jnp.logical_or, [role == at for at in HELD_BACK])
    left_out = functools.reduce(lambda n, r: jnp.where(role == r, HELD_BACK[r], n), HELD_BACK, 0)

    def remote(src, dst, send, recv, to):
        return pltpu.make_async_remote_copy(
            src_ref=src, dst_ref=dst, send_sem=send, recv_sem=recv, device_id=to, device_id_type=MESH
        )

    def unit(src, at, p, to):
        recv = jnp.where(at < WHOLE, (at - NEAR) * patches + p, (WHOLE - NEAR) * patches + at - WHOLE)
        return remote(spec.at[src, p], spec.at[at, p], unit_send.at[0], spec_recv.at[recv], to)

    def arrival(at, p):
        return unit(at, at, p, device(-1))

    def arrival_of_look(at):
        recv = (WHOLE - NEAR) * patches + at - WHOLE
        return remote(spec.at[at], spec.at[at], unit_send.at[0], spec_recv.at[recv], device(-1))

    def to_near(look, p):
        meeting = jnp.logical_or(me == 0, me == half)
        to = jnp.where(meeting, hub, lax.rem(me - 1 + nlook, nlook))
        at = jnp.where(me == 0, LOW, jnp.where(me == half, HIGH, NEAR)) + look
        return unit(OWN + look, at, p, (to, lane))

    def to_far(look, p):
        meeting = jnp.logical_or(look == 1, jnp.logical_or(me == 1, me == half + 1))
        to = jnp.where(meeting, hub, lax.rem(me - 2 + nlook, nlook))
        at = jnp.where(me == 1, LOW + 2, jnp.where(me == half + 1, HIGH + 2, FAR))
        at = jnp.where(look == 1, LAST + 2, at)
        return unit(OWN + look, at, p, (to, lane))

    def to_opp(look, p):
        return unit(OWN + look, OPP + look, p, device(half))

    def relayed(b, p, mate, at):
        to = jnp.where(mate, lax.rem(me - 1 + nlook, nlook), half - 1)
        return unit(b, at, p, (to, lane))

    def each_send(look, p):
        has_far = jnp.logical_and(odd == 1, jnp.logical_or(look == 0, me == half - 1))
        has_opp = jnp.where(look == 0, bit(sents, 0), bit(sents, 1))

        @pl.when(jnp.logical_and(has_opp, jnp.logical_not(late)))
        def _():
            to_opp(look, p).start()

        held = jnp.logical_and(role == LATE_NEAR, look == 0)

        @pl.when(jnp.logical_not(held))
        def _():
            to_near(look, p).start()

        @pl.when(has_far)
        def _():
            to_far(look, p).start()

    for look in range(looks):
        energy[look] = jnp.zeros((8, 128), jnp.float32)

    def forward(u, carry):
        @pl.when(u == 1)
        def _():
            pl.semaphore_wait(barrier, expected - missing)
            for later, to in behind:

                @pl.when(later)
                def _():
                    pl.semaphore_signal(ready, inc=1, device_id=to, device_id_type=MESH)

        @pl.when(u > 0)
        def _():
            each_send(look_at(u - 1), (u - 1) % patches)

        look, p = look_at(u), u % patches
        load(u).wait()

        @pl.when(u < units - AHEAD)
        def _():
            load(u + AHEAD).start()

        @pl.when(u == units - AHEAD)
        def _():
            tables[2].start()
            tables[3].start()

        spec_even, spec_odd = spectrum_of(img.at[u], left_ref, right_ref)
        quarter = BAND // 2
        spec[OWN + look, p, 0, :, :quarter] = spec_even[:, :quarter]
        spec[OWN + look, p, 0, :, quarter:] = spec_odd[:, :quarter]
        spec[OWN + look, p, 1, :, :quarter] = spec_even[:, quarter:]
        spec[OWN + look, p, 1, :, quarter:] = spec_odd[:, quarter:]
        energy[look] += w_ref[p] * squares_of(spec_even, spec_odd)
        return carry

    tables[0].wait()
    tables[1].wait()
    lax.fori_loop(0, units, forward, 0)
    each_send(look_at(units - 1), (units - 1) % patches)

    tell = []
    for d, look_by in enumerate((0, 1, 2, half)):
        for by in range(nswath):
            if look_by or by:
                tell.append(remote(energy, heard.at[d * nswath + by], heard_send.at[0], heard_recv.at[0],
                                   device(-look_by, by)))

    @pl.when(me < 2)
    def _():
        pl.semaphore_wait(ready, missing)

    for copy in tell:
        copy.start()

    lists = [coded(steps) for steps in step_lists()]
    count = pick(role, [len(steps) for steps in lists])
    backs = pick(role, [sum(2**at for at in outs) for outs in BACK])
    dos, ends = (
        [pick(role, [steps[i][which] if i < len(steps) else 0 for steps in lists]) for i in range(STEPS)]
        for which in (0, 1)
    )

    rows = WIN // nswath
    mine = pl.ds(pl.multiple_of(lane * rows, rows), rows)

    def outgoing(slot, by):
        at = pl.ds(pl.multiple_of(lax.rem(lane + by, nswath) * rows, rows), rows)
        return remote(outbox.at[slot, at], inbox.at[by - 1, slot], box_send.at[by - 1],
                      box_recv.at[by - 1, slot], device(0, by))

    def part(slot, by):
        at = pl.ds(pl.multiple_of(lax.rem(lane + by, nswath) * rows, rows), rows)
        return remote(outbox.at[slot, at], parts.at[by], parts_send.at[0], parts_recv.at[0], device(half, by))

    def returned(slot, to, out):
        where = pick(to, [me, lax.rem(me + half, nlook), half - 2, half - 1, 0, 1, half, half + 1])
        return remote(turned.at[slot], backbox.at[out], back_send.at[0], back_recv.at[out], (where, lane))

    def finish(i, at, slot, to, out):
        value = surf[at, mine, :]
        for by in range(1, nswath):
            outgoing(slot, by).wait_recv()
            value = value + inbox[by - 1, slot].astype(jnp.float32)

        @pl.when(to == HERE)
        def _():
            final[out] = value
            put(out).start()

        @pl.when(to != HERE)
        def _():
            turned[slot] = value.astype(jnp.bfloat16)

            @pl.when(jnp.logical_not(jnp.logical_and(held_back, i < count - left_out)))
            def _():
                returned(slot, to, out).start()

    def send_late(p):
        @pl.when(role == LATE_NEAR)
        def _():
            to_near(0, p).start()

        @pl.when(role != LATE_NEAR)
        def _():
            to_opp(1, p).start()

    def put(out):
        return pltpu.make_async_copy(final.at[out], out_hbm.at[out], out_sem.at[0])

    put_factor = pltpu.make_async_copy(factors, factor_hbm, table_sem.at[0])

    tables[2].wait()
    tables[3].wait()

    def step(i, carry):
        a, b, wait_a, wait_b, compute, back, relay, relay_at, now, flush, direct, slot = decode(pick(i, dos), DO_BASES)

        @pl.when(flush == 1)
        def _():
            for at, code in enumerate(carry):
                settle(i - LAG + at, code)

        carry = tuple(jnp.where(flush == 1, 0, code) for code in carry)

        @pl.when(i == count - 1)
        def _():
            weigh()

        @pl.when(jnp.logical_and(compute == 0, wait_b == 0))
        def _():
            arrival(b, a).wait_recv()
            relayed(b, a, relay == TO_MATE, relay_at).start()

        @pl.when(wait_a == 1)
        def _():
            arrival_of_look(a).wait_recv()

        @pl.when(jnp.logical_and(wait_b == 1, b >= WHOLE))
        def _():
            arrival_of_look(b).wait_recv()

        @pl.when(jnp.logical_and(wait_b == 1, b < WHOLE))
        def _():
            for p in range(patches):
                arrival(b, p).wait_recv()

                @pl.when(relay != 0)
                def _():
                    relayed(b, p, relay == TO_MATE, relay_at).start()

                if p >= patches - 2:

                    @pl.when(jnp.logical_and(now == 1, (role == LATE_NEAR) == (p == patches - 1)))
                    def _():
                        for q in range(patches):
                            send_late(q)

        @pl.when(jnp.logical_and(held_back, i == count - 1))
        def _():
            release()

        @pl.when(compute == 1)
        def _():
            cross_into(w_ref, spec.at[a], spec.at[b], cre, cim)
            keep, turn = halves(first_ref, second_ref, cre, cim)
            value = keep - turn
            surf[i % HELD] = value
            outbox[slot] = value.astype(jnp.bfloat16)
            value = keep + turn
            surf[HELD + i % HELD] = value
            for by in range(1, nswath):
                outgoing(slot, by).start()

            @pl.when(back == 1)
            def _():
                outbox[slot + 1] = value.astype(jnp.bfloat16)

                @pl.when(direct == 1)
                def _():
                    for by in range(nswath):
                        part(slot + 1, by).start()

                @pl.when(direct == 0)
                def _():
                    for by in range(1, nswath):
                        outgoing(slot + 1, by).start()

        settle(i - LAG, carry[0])
        return (*carry[1:], pick(i, ends))

    def release():
        pl.semaphore_wait(go, 1)
        for r, leaves in HELD_BACK.items():

            @pl.when(role == r)
            def _():
                slot = 0
                for do, end in step_lists()[r][:-leaves]:
                    if do[4] and end[2] != HERE:
                        returned(slot, jnp.int32(end[2]), end[3]).start()
                    if end[1]:
                        returned(slot + 1, jnp.int32(end[4]), end[5]).start()
                    slot += do[4] + do[5]

    def settle(i, code):
        compute, back, to, out, back_to, back_out, slot = decode(code, END_BASES)

        @pl.when(compute == 1)
        def _():
            at = lax.rem(i + HELD, HELD)

            @pl.when(back == 1)
            def _():
                finish(i, HELD + at, slot + 1, back_to, back_out)

            finish(i, at, slot, to, out)

    def all_heard():
        told = heard.at[pl.ds(1, 4 * nswath - 1)]
        return remote(told, told, heard_send.at[0], heard_recv.at[0], device(-1))

    def weigh():
        all_heard().wait_recv()
        total = []
        for d in range(4):
            for look in range(looks):
                parts = energy[look] if d == 0 else heard[d * nswath, look]
                for by in range(1, nswath):
                    parts = parts + heard[d * nswath + by, look]
                total.append(jnp.sum(parts, axis=(0, 1), keepdims=True))
        scale = BAND * math.sqrt(patches * nswath)

        def factor(look, lag):
            mate = total[look + lag + 1] if lag < 3 else total[3 * looks + look]
            return mask_ref[look, lag].astype(jnp.float32) * scale / jnp.sqrt(total[look] * mate)

        for look in range(looks):
            for lag in range(4):
                factors[look, lag : lag + 1, :] = jnp.broadcast_to(factor(look, lag), (1, WIN))
        put_factor.start()

    def fetch(out, carry):
        @pl.when(bit_of(backs, out))
        def _():
            remote(turned.at[0], backbox.at[out], back_send.at[0], back_recv.at[out], device(half)).wait_recv()
            final[out] = backbox[out].astype(jnp.float32)
            put(out).start()

        return carry

    def bit_of(mask, at):
        return pick(at, [lax.rem(lax.div(mask, jnp.int32(2**k)), 2) for k in range(OUTS)]) == 1

    def by_role(counts, act):
        mine_of = pick(role, list(counts))
        for n in sorted(set(counts)):
            if n:

                @pl.when(mine_of == n)
                def _():
                    act(n)

    def drain_units(n):
        sent = spec.at[pl.ds(0, n)]
        remote(sent, sent, unit_send.at[0], spec_recv.at[0], device(-1)).wait_send()

    def drain_boxes(n):
        for by in range(1, nswath):
            sent = inbox.at[by - 1, pl.ds(0, n)]
            remote(sent, sent, box_send.at[by - 1], box_recv.at[by - 1, 0], device(0, by)).wait_send()

    def drain_returns(n):
        sent = turned.at[pl.ds(0, n)]
        remote(sent, sent, back_send.at[0], back_recv.at[0], device(half)).wait_send()

    pending = lax.fori_loop(0, count, step, (jnp.int32(0),) * LAG)
    for at, code in enumerate(pending):
        settle(count - LAG + at, code)
    by_role([looks_sent(r, patches) for r in range(len(RESULTS))], drain_units)

    @pl.when(functools.reduce(jnp.logical_or, [role == at for at in FREES]))
    def _():
        to = jnp.where(odd == 1, me - 1, me + 1)
        pl.semaphore_signal(go, inc=1, device_id=(to, lane), device_id_type=MESH)

    lax.fori_loop(0, OUTS, fetch, 0)
    place_of = pick(role, [PARTS_OF.get(r, OUTS) for r in range(len(RESULTS))])
    all_parts = remote(parts, parts, parts_send.at[0], parts_recv.at[0], device(half))

    @pl.when(place_of < OUTS)
    def _():
        all_parts.wait_recv()
        value = parts[0].astype(jnp.float32)
        for by in range(1, nswath):
            value = value + parts[by].astype(jnp.float32)
        final[place_of] = value
        put(place_of).start()

    @pl.when(functools.reduce(jnp.logical_or, [role == r for r in PARTS_BY]))
    def _():
        all_parts.wait_send()

    by_role(RESULTS, drain_boxes)
    by_role(RETURNS, drain_returns)
    all_heard().wait_send()
    put_factor.wait()
    pltpu.make_async_copy(final, out_hbm, out_sem.at[0]).wait()


def per_device(images, patch_weight, pair_mask):
    nlook = lax.axis_size("look")
    nswath = lax.axis_size("swath")
    looks, patches = images.shape[:2]
    left, right = forward_tables()
    first, second = inverse_tables()
    rows = WIN // nswath
    hbm = pl.BlockSpec(memory_space=pltpu.HBM)
    smem = pl.BlockSpec(memory_space=pltpu.SMEM)
    dma = pltpu.SemaphoreType.DMA
    unit = (2, BAND, BAND)
    others = max(nswath - 1, 1)
    operands = (patch_weight, pair_mask, images, left, right, first, second)
    surfaces, scales = pl.pallas_call(
        functools.partial(kernel, nlook, nswath),
        in_specs=[smem, smem] + [hbm] * 5,
        out_specs=[pl.BlockSpec(memory_space=pl.ANY)] * 2,
        out_shape=[
            jax.ShapeDtypeStruct((OUTS, rows, WIN), jnp.float32),
            jax.ShapeDtypeStruct((looks, 4, WIN), jnp.float32),
        ],
        scratch_shapes=[
            pltpu.VMEM(left.shape, jnp.bfloat16),
            pltpu.VMEM(right.shape, jnp.bfloat16),
            pltpu.VMEM(first.shape, jnp.bfloat16),
            pltpu.VMEM(second.shape, jnp.bfloat16),
            pltpu.VMEM((looks * patches, 2, PIX, PIX), jnp.bfloat16),
            pltpu.VMEM((BUFFERS, patches) + unit, jnp.bfloat16),
            pltpu.VMEM((looks, 8, 128), jnp.float32),
            pltpu.VMEM((4 * nswath, looks, 8, 128), jnp.float32),
            pltpu.VMEM((BAND, BAND), jnp.bfloat16),
            pltpu.VMEM((BAND, BAND), jnp.bfloat16),
            pltpu.VMEM((2 * HELD, WIN, WIN), jnp.float32),
            pltpu.VMEM((SLOTS, WIN, WIN), jnp.bfloat16),
            pltpu.VMEM((others, SLOTS, rows, WIN), jnp.bfloat16),
            pltpu.VMEM((SLOTS, rows, WIN), jnp.bfloat16),
            pltpu.VMEM((OUTS, rows, WIN), jnp.bfloat16),
            pltpu.VMEM((nswath, rows, WIN), jnp.bfloat16),
            pltpu.VMEM((OUTS, rows, WIN), jnp.float32),
            pltpu.VMEM((looks, 4, WIN), jnp.float32),
            dma((4,)),
            dma((AHEAD,)),
            dma((1,)),
            dma(((WHOLE - NEAR) * patches + BUFFERS - WHOLE,)),
            dma((1,)),
            dma((1,)),
            dma((others,)),
            dma((others, SLOTS)),
            dma((1,)),
            dma((OUTS,)),
            dma((1,)),
            dma((1,)),
            dma((1,)),
            pltpu.SemaphoreType.REGULAR,
            pltpu.SemaphoreType.REGULAR,
        ],
        compiler_params=pltpu.CompilerParams(
            collective_id=0, has_side_effects=True, vmem_limit_bytes=52224 << 10
        ),
        name="autofocus",
    )(*[pltpu.with_memory_space_constraint(x, pltpu.HBM) for x in operands])
    return surfaces.reshape(looks, 4, rows, WIN) * scales[:, :, None, :]


def solution(mesh):
    return jax.shard_map(
        per_device,
        mesh=mesh,
        in_specs=(P("look", "swath", None, None, None), P("swath"), P("look", None)),
        out_specs=P("look", None, "swath", None),
        check_vma=False,
    )
```

```python
import functools
import math

import jax
import jax.numpy as jnp
import numpy as np
from jax import lax
from jax.experimental import pallas as pl
from jax.experimental.pallas import tpu as pltpu
from jax.sharding import PartitionSpec as P

PIX = 512
BAND = 256
WIN = 256
HALF = PIX // 2


def phases(rows, cols, row_shift, col_shift):
    phase = (rows[:, None] - row_shift) * (cols[None, :] - col_shift) % PIX
    angle = 2.0 * math.pi / PIX * phase
    return np.cos(angle), np.sin(angle)


def forward_tables():
    left, right = [], []
    for parity in (0, 1):
        re, im = phases(np.arange(parity, BAND, 2), np.arange(HALF), BAND // 2, 0)
        im = -im
        left.append(np.block([[re, -im], [im, re]]))
        right.append(np.block([[re.T, im.T], [-im.T, re.T]]))
    return jnp.asarray(np.stack(left), jnp.bfloat16), jnp.asarray(np.stack(right), jnp.bfloat16)


def inverse_tables():
    order = np.concatenate([np.arange(0, BAND, 2), np.arange(1, BAND, 2)])
    re, im = phases(np.arange(WIN), order, WIN // 2, BAND // 2)
    first = np.concatenate([re, im], axis=0)
    second = np.stack([re.T, im.T])
    return jnp.asarray(first, jnp.bfloat16), jnp.asarray(second, jnp.bfloat16)


def dot(left, right):
    return jnp.dot(left, right, preferred_element_type=jnp.float32)


ROWS = 32
MESH = pl.DeviceIdType.MESH


def spectrum_of(img, left_ref, right_ref):
    re0, re1 = img[0, :HALF, :], img[0, HALF:, :]
    im0, im1 = img[1, :HALF, :], img[1, HALF:, :]
    even = dot(left_ref[0], jnp.concatenate([re0 + re1, im0 + im1], axis=0))
    odd = dot(left_ref[1], jnp.concatenate([re0 - re1, im0 - im1], axis=0))
    quarter = BAND // 2
    parts = []
    for at in (0, quarter):
        parts.append(jnp.concatenate([even[at : at + quarter], odd[at : at + quarter]], axis=0))
    plus = [(part[:, :HALF] + part[:, HALF:]).astype(jnp.bfloat16) for part in parts]
    minus = [(part[:, :HALF] - part[:, HALF:]).astype(jnp.bfloat16) for part in parts]
    spec_even = dot(jnp.concatenate(plus, axis=1), right_ref[0]).astype(jnp.bfloat16)
    spec_odd = dot(jnp.concatenate(minus, axis=1), right_ref[1]).astype(jnp.bfloat16)
    return spec_even, spec_odd


def squares_of(spec_even, spec_odd):
    total = spec_even.astype(jnp.float32) ** 2 + spec_odd.astype(jnp.float32) ** 2
    folded = jnp.sum(total.reshape(BAND // 8, 8, BAND), axis=0)
    return folded[:, : BAND // 2] + folded[:, BAND // 2 :]


def cross_into(w_ref, a_ref, b_ref, cre, cim):
    patches = a_ref.shape[0]

    def step(i, carry):
        rows = pl.ds(pl.multiple_of(i * ROWS, ROWS), ROWS)
        re = jnp.zeros((ROWS, BAND), jnp.float32)
        im = jnp.zeros((ROWS, BAND), jnp.float32)
        for p in range(patches):
            weight = w_ref[p]
            ar = a_ref[p, 0, rows, :].astype(jnp.float32) * weight
            ai = a_ref[p, 1, rows, :].astype(jnp.float32) * weight
            br = b_ref[p, 0, rows, :].astype(jnp.float32)
            bi = b_ref[p, 1, rows, :].astype(jnp.float32)
            re += ar * br + ai * bi
            im += ai * br - ar * bi
        cre[rows, :] = re.astype(jnp.bfloat16)
        cim[rows, :] = im.astype(jnp.bfloat16)
        return carry

    lax.fori_loop(0, BAND // ROWS, step, 0)


def add_patch(w_ref, a_ref, b_ref, p, acc, cre=None, cim=None):
    def step(i, carry):
        rows = pl.ds(pl.multiple_of(i * ROWS, ROWS), ROWS)
        weight = w_ref[p]
        ar = a_ref[p, 0, rows, :].astype(jnp.float32) * weight
        ai = a_ref[p, 1, rows, :].astype(jnp.float32) * weight
        br = b_ref[p, 0, rows, :].astype(jnp.float32)
        bi = b_ref[p, 1, rows, :].astype(jnp.float32)
        re = ar * br + ai * bi
        im = ai * br - ar * bi
        if p:
            re = acc[0, rows, :] + re
            im = acc[1, rows, :] + im
        if cre is None:
            acc[0, rows, :] = re
            acc[1, rows, :] = im
        else:
            cre[rows, :] = re.astype(jnp.bfloat16)
            cim[rows, :] = im.astype(jnp.bfloat16)
        return carry

    lax.fori_loop(0, BAND // ROWS, step, 0)


def halves(first_ref, second_ref, cre, cim):
    from_re = dot(first_ref[...], cre[...]).astype(jnp.bfloat16)
    from_im = dot(first_ref[...], cim[...]).astype(jnp.bfloat16)
    keep = dot(from_re[:WIN], second_ref[0]) - dot(from_re[WIN:], second_ref[1])
    turn = dot(from_im[:WIN], second_ref[1]) + dot(from_im[WIN:], second_ref[0])
    return keep, turn


OWN, NEAR, FAR, LOW, OPP, LAST, HIGH = 0, 2, 4, 5, 5, 8, 11
BUFFERS = 14
WHOLE = LAST
OUTS = 8
HERE, ACROSS, LAST_EVEN, LAST_ODD, ZERO, ONE, HALF_EVEN, HALF_ODD = range(8)
TO_MATE, TO_LAST = 1, 2


def pair_step(a, b, out, to=HERE, wait_a=False, wait_b=False, back=None, relay=(0, 0), compute=True, late=False,
              flush=False, direct=False, adds=0, ends=0):
    back_to, back_out = back if back else (HERE, 0)
    do = (a, b, int(wait_a), int(wait_b), int(compute), int(back is not None), relay[0], relay[1], int(late),
          int(flush), int(direct), adds, ends)
    end = (int(compute), int(back is not None and not direct), to, out, back_to, back_out)
    return do, end


DO_BASES = (16, 16, 2, 2, 2, 2, 4, 16, 2, 2, 2, 4, 4, 32)
END_BASES = (2, 2, 8, 8, 8, 8, 32)


def encode(values, bases):
    code = 0
    for value, base in zip(reversed(values), reversed(bases), strict=True):
        code = code * base + value
    return code


def decode(code, bases):
    values = []
    for base in bases:
        values.append(lax.rem(code, base))
        code = lax.div(code, base)
    return values


def coded(steps):
    codes, slot = [], 0
    for do, end in steps:
        codes.append((encode(do + (slot,), DO_BASES), encode(end + (slot,), END_BASES)))
        slot += do[4] + do[5]
    return codes


def relay_step(b, relay):
    return pair_step(0, b, 0, wait_b=True, relay=relay, compute=False)


def relay_unit(b, p, relay):
    return pair_step(p, b, 0, relay=relay, compute=False)


def opposite(k, direct=False, flush=False):
    out = 4 * k + 3
    return pair_step(OWN + k, OPP + k, out, wait_b=True, back=(ACROSS, out), direct=direct, flush=flush,
                     adds=int(direct), ends=int(direct))


def step_lists():
    first = [pair_step(OWN, OWN + 1, 0)]
    near_pairs = [
        pair_step(OWN, NEAR, 1, wait_b=True),
        pair_step(OWN + 1, NEAR, 4),
        pair_step(OWN, NEAR + 1, 2, wait_b=True),
        pair_step(OWN + 1, NEAR + 1, 5),
    ]
    on_chip = first + near_pairs
    even = on_chip + [pair_step(OWN + 1, FAR, 6, wait_b=True)]
    to_far = (TO_MATE, FAR)

    def odd(end, late=False):
        return (
            first
            + [
                pair_step(OWN, NEAR, 1, wait_b=True, relay=to_far),
                pair_step(OWN + 1, NEAR, 4),
                pair_step(OWN + 1, FAR, 6, wait_b=True),
                pair_step(OWN, NEAR + 1, 2, wait_b=True, late=late),
                pair_step(OWN + 1, NEAR + 1, 5),
            ]
            + end
        )

    def pass_on(p, which):
        at = (NEAR, NEAR + 1, FAR)[which]
        return relay_unit(LOW + which, p, (TO_LAST, at))

    def pass_both(p):
        return [pass_on(p, 0), pass_on(p, 2)]

    hub = (
        pass_both(0)
        + first
        + near_pairs[:2]
        + pass_both(1)
        + near_pairs[2:]
        + pass_both(2)
        + pass_both(3)
        + [
            pair_step(LOW, HIGH, 3, ZERO, wait_b=True, back=(HALF_EVEN, 3)),
            pass_on(0, 1),
            pair_step(LOW + 2, HIGH + 2, 3, ONE, wait_b=True, back=(HALF_ODD, 3)),
            pass_on(1, 1),
            pass_on(2, 1),
            pair_step(LAST, HIGH, 6, LAST_EVEN, wait_a=True),
            pass_on(3, 1),
            pair_step(LAST + 2, HIGH, 4, LAST_ODD, wait_a=True),
            pair_step(LAST + 2, HIGH + 2, 6, LAST_ODD),
            pair_step(LOW + 1, HIGH + 1, 7, ZERO, wait_b=True, back=(HALF_EVEN, 7)),
            pair_step(LAST + 2, HIGH + 1, 5, LAST_ODD),
            pair_step(LAST + 1, HIGH, 1, LAST_ODD, wait_a=True),
            pair_step(LAST + 1, HIGH + 1, 2, LAST_ODD),
            pair_step(OWN + 1, FAR, 6, wait_b=True, flush=True, adds=1, ends=1),
        ]
    )
    hub_odd = first + [
        pair_step(OWN, NEAR + 1, 2, wait_b=True, relay=(TO_MATE, LAST)),
        pair_step(OWN + 1, NEAR + 1, 5),
        pair_step(OWN + 1, FAR, 6, wait_b=True, relay=(TO_MATE, LAST + 1)),
        pair_step(OWN, NEAR, 1, wait_b=True, relay=to_far, adds=2, ends=1),
        pair_step(OWN + 1, OPP + 1, 7, wait_b=True, back=(ACROSS, 7), direct=True),
        pair_step(OWN + 1, NEAR, 4, ends=2),
    ]
    last_even = on_chip + [
        opposite(1),
        pair_step(0, FAR, 0, wait_b=True, compute=False, late=True),
        pair_step(OPP + 1, FAR, 6, ACROSS),
    ]
    last_odd = first + [
        relay_step(NEAR, to_far),
        opposite(0),
        pair_step(OPP, NEAR, 1, ACROSS),
        opposite(1),
        pair_step(OPP + 1, NEAR, 4, ACROSS),
        pair_step(OPP + 1, FAR, 6, ACROSS, wait_b=True),
        pair_step(OPP, NEAR + 1, 2, ACROSS, wait_b=True, flush=True),
        pair_step(OPP + 1, NEAR + 1, 5, ACROSS),
    ]
    return (
        even,
        odd([], late=True),
        even,
        odd([opposite(1, True)]),
        hub,
        hub_odd,
        last_even,
        last_odd,
        even,
        odd([opposite(1, True)]),
        even + [opposite(0), opposite(1, True, True)],
        odd([opposite(0)], late=True),
        on_chip + [opposite(0, True)],
        first,
    )


BACK = ((3, 7), (3,), (3,), (3,), (3,), (3,), (6,), (1, 2, 4, 5, 6), (3, 7), (3,), (), (), (6, 7), (1, 2, 3, 4, 5, 6, 7))
PARTS_OF = {1: 7, 2: 7, 4: 7, 6: 3, 11: 7}
PARTS_BY = (3, 5, 9, 10, 12)
HELD_BACK, FREES = {7: 2, 10: 1}, (6, 11)
SENT = ((), (1,), (0, 1), (0,), (0, 1), (0,), (0,), (), (), (), (), (1,), (1,), (0, 1))
LATE, LATE_NEAR = (1, 11), 6
AHEAD = 2
LAG = 2
HELD = 4
STEPS = max(len(steps) for steps in step_lists())
RESULTS = [sum(end[0] + end[1] for _, end in steps) for steps in step_lists()]
RETURNS = [sum(int(end[2] != HERE) + end[1] for _, end in steps) for steps in step_lists()]
SLOTS = max(sum(do[4] + do[5] for do, _ in steps) for steps in step_lists())


def looks_sent(role, patches):
    relayed = sum((patches if do[3] else 1) for do, _ in step_lists()[role] if do[6])
    return 2 + role % 2 + int(role == 7) + len(SENT[role]) + relayed // patches


def pick(index, values):
    result = jnp.int32(values[0]) if isinstance(values[0], int) else values[0]
    for at, value in enumerate(values[1:], 1):
        result = jnp.where(index == at, value, result)
    return result


def bit(mask, at):
    return lax.rem(lax.div(mask, jnp.int32(2**at)), 2) == 1


def kernel(nlook, nswath, w_ref, mask_ref, img_ref, left_hbm, right_hbm, first_hbm, second_hbm, out_hbm, factor_hbm,
           left_ref, right_ref, first_ref, second_ref, img, spec, energy, heard, cre, cim, acc, surf, outbox, inbox, turned, backbox, parts, final, factors,
           table_sem, img_sem, unit_send, spec_recv,
           heard_send, heard_recv, box_send, box_recv, back_send, back_recv, parts_send, parts_recv, out_sem, ready, go):
    looks, patches = img_ref.shape[:2]
    half = nlook // 2
    hub = half - 4
    me, lane = lax.axis_index("look"), lax.axis_index("swath")
    chip, odd = lax.div(me, 2), lax.rem(me, 2)
    lead = jnp.where(chip == half // 2 - 1, 1, 0)

    def device(look_by, swath_by=0):
        return (lax.rem(me + look_by + nlook, nlook), lax.rem(lane + swath_by, nswath))

    def look_at(u):
        return lax.rem(lead + u // patches, looks)

    def load(u):
        return pltpu.make_async_copy(img_ref.at[look_at(u), u % patches], img.at[u], img_sem.at[u % AHEAD])

    tables = [
        pltpu.make_async_copy(src, dst, table_sem.at[i % 2])
        for i, (src, dst) in enumerate(
            ((left_hbm, left_ref), (right_hbm, right_ref), (first_hbm, first_ref), (second_hbm, second_ref))
        )
    ]
    barrier = pltpu.get_barrier_semaphore()
    behind = []

    def greet(look_bys):
        count = 0
        for look_by in look_bys:
            for by in range(nswath):
                if look_by or by:
                    count += 1
                    to = device(look_by, by)
                    if look_by in (1, 2, half):
                        ends_of_low = jnp.logical_or(to[0] < 2, jnp.logical_and(to[0] >= half - 2, to[0] < half))
                        later = jnp.logical_and(ends_of_low, me >= half)
                        behind.append((later, to))

                        @pl.when(jnp.logical_not(later))
                        def _():
                            pl.semaphore_signal(barrier, inc=1, device_id=to, device_id_type=MESH)
                    else:
                        pl.semaphore_signal(barrier, inc=1, device_id=to, device_id_type=MESH)
        return count

    greeted = greet((half,))
    units = looks * patches
    load(0).start()
    tables[0].start()
    tables[1].start()
    greeted += greet((0, 1, -1, 2, -2))
    met = (0, 1, half - 1, half, half + 1)
    meets = functools.reduce(jnp.logical_or, [me == at for at in met])

    @pl.when(me == hub)
    def _():
        for at in met:
            pl.semaphore_signal(barrier, inc=1, device_id=(jnp.int32(at), lane), device_id_type=MESH)

    @pl.when(meets)
    def _():
        pl.semaphore_signal(barrier, inc=1, device_id=(jnp.int32(hub), lane), device_id_type=MESH)

    expected = jnp.where(me == hub, greeted + len(met), jnp.where(meets, greeted + 1, greeted))
    on_last = chip == half // 2 - 1
    missing = jnp.where(me == 0, 3 * nswath, jnp.where(me == 1, 2 * nswath, jnp.where(on_last, nswath, 0)))

    place = jnp.where(me < half, jnp.int32(1), jnp.int32(5))
    for at, value in ((0, 0), (half // 2 - 2, 2), (half // 2 - 1, 3), (half // 2, 4), (half - 1, 6)):
        place = jnp.where(chip == at, value, place)
    role = 2 * place + odd
    sents = pick(role, [sum(2**at for at in ks) for ks in SENT])
    late = jnp.logical_or(role == LATE[0], jnp.logical_and(role == LATE[1], chip >= half // 2 + 2))
    held_back = functools.reduce(jnp.logical_or, [role == at for at in HELD_BACK])
    left_out = functools.reduce(lambda n, r: jnp.where(role == r, HELD_BACK[r], n), HELD_BACK, 0)

    def remote(src, dst, send, recv, to):
        return pltpu.make_async_remote_copy(
            src_ref=src, dst_ref=dst, send_sem=send, recv_sem=recv, device_id=to, device_id_type=MESH
        )

    def unit(src, at, p, to):
        recv = jnp.where(at < WHOLE, (at - NEAR) * patches + p, (WHOLE - NEAR) * patches + at - WHOLE)
        return remote(spec.at[src, p], spec.at[at, p], unit_send.at[0], spec_recv.at[recv], to)

    def arrival(at, p):
        return unit(at, at, p, device(-1))

    def arrival_of_look(at):
        recv = (WHOLE - NEAR) * patches + at - WHOLE
        return remote(spec.at[at], spec.at[at], unit_send.at[0], spec_recv.at[recv], device(-1))

    def to_near(look, p):
        meeting = jnp.logical_or(me == 0, me == half)
        to = jnp.where(meeting, hub, lax.rem(me - 1 + nlook, nlook))
        at = jnp.where(me == 0, LOW, jnp.where(me == half, HIGH, NEAR)) + look
        return unit(OWN + look, at, p, (to, lane))

    def to_far(look, p):
        meeting = jnp.logical_or(look == 1, jnp.logical_or(me == 1, me == half + 1))
        to = jnp.where(meeting, hub, lax.rem(me - 2 + nlook, nlook))
        at = jnp.where(me == 1, LOW + 2, jnp.where(me == half + 1, HIGH + 2, FAR))
        at = jnp.where(look == 1, LAST + 2, at)
        return unit(OWN + look, at, p, (to, lane))

    def to_opp(look, p):
        return unit(OWN + look, OPP + look, p, device(half))

    def relayed(b, p, mate, at):
        to = jnp.where(mate, lax.rem(me - 1 + nlook, nlook), half - 1)
        return unit(b, at, p, (to, lane))

    def each_send(look, p):
        has_far = jnp.logical_and(odd == 1, jnp.logical_or(look == 0, me == half - 1))
        has_opp = jnp.where(look == 0, bit(sents, 0), bit(sents, 1))

        @pl.when(jnp.logical_and(has_opp, jnp.logical_not(late)))
        def _():
            to_opp(look, p).start()

        held = jnp.logical_and(role == LATE_NEAR, look == 0)

        @pl.when(jnp.logical_not(held))
        def _():
            to_near(look, p).start()

        @pl.when(has_far)
        def _():
            to_far(look, p).start()

    for look in range(looks):
        energy[look] = jnp.zeros((8, 128), jnp.float32)

    def forward(u, carry):
        @pl.when(u == 1)
        def _():
            pl.semaphore_wait(barrier, expected - missing)
            for later, to in behind:

                @pl.when(later)
                def _():
                    pl.semaphore_signal(ready, inc=1, device_id=to, device_id_type=MESH)

        @pl.when(jnp.logical_and(on_last, u == patches + 1))
        def _():
            pl.semaphore_wait(ready, missing)

        @pl.when(u > 0)
        def _():
            each_send(look_at(u - 1), (u - 1) % patches)

        look, p = look_at(u), u % patches
        load(u).wait()

        @pl.when(u == 0)
        def _():
            for first in range(1, AHEAD):
                load(first).start()

        @pl.when(u < units - AHEAD)
        def _():
            load(u + AHEAD).start()

        @pl.when(u == units - AHEAD)
        def _():
            tables[2].start()
            tables[3].start()

        spec_even, spec_odd = spectrum_of(img.at[u], left_ref, right_ref)
        quarter = BAND // 2
        spec[OWN + look, p, 0, :, :quarter] = spec_even[:, :quarter]
        spec[OWN + look, p, 0, :, quarter:] = spec_odd[:, :quarter]
        spec[OWN + look, p, 1, :, :quarter] = spec_even[:, quarter:]
        spec[OWN + look, p, 1, :, quarter:] = spec_odd[:, quarter:]
        energy[look] += w_ref[p] * squares_of(spec_even, spec_odd)
        return carry

    tables[0].wait()
    tables[1].wait()
    lax.fori_loop(0, units, forward, 0)
    each_send(look_at(units - 1), (units - 1) % patches)

    tell = []
    for d, look_by in enumerate((0, 1, 2, half)):
        for by in range(nswath):
            if look_by or by:
                tell.append(remote(energy, heard.at[d * nswath + by], heard_send.at[0], heard_recv.at[0],
                                   device(-look_by, by)))

    @pl.when(me < 2)
    def _():
        pl.semaphore_wait(ready, missing)

    for copy in tell:
        copy.start()

    lists = [coded(steps) for steps in step_lists()]
    count = pick(role, [len(steps) for steps in lists])
    backs = pick(role, [sum(2**at for at in outs) for outs in BACK])
    dos, ends = (
        [pick(role, [steps[i][which] if i < len(steps) else 0 for steps in lists]) for i in range(STEPS)]
        for which in (0, 1)
    )

    rows = WIN // nswath
    mine = pl.ds(pl.multiple_of(lane * rows, rows), rows)

    def outgoing(slot, by):
        at = pl.ds(pl.multiple_of(lax.rem(lane + by, nswath) * rows, rows), rows)
        return remote(outbox.at[slot, at], inbox.at[by - 1, slot], box_send.at[by - 1],
                      box_recv.at[by - 1, slot], device(0, by))

    def part(slot, by):
        at = pl.ds(pl.multiple_of(lax.rem(lane + by, nswath) * rows, rows), rows)
        return remote(outbox.at[slot, at], parts.at[by], parts_send.at[0], parts_recv.at[0], device(half, by))

    def returned(slot, to, out):
        where = pick(to, [me, lax.rem(me + half, nlook), half - 2, half - 1, 0, 1, half, half + 1])
        return remote(turned.at[slot], backbox.at[out], back_send.at[0], back_recv.at[out], (where, lane))

    def finish(i, at, slot, to, out):
        value = surf[at, mine, :]
        for by in range(1, nswath):
            outgoing(slot, by).wait_recv()
            value = value + inbox[by - 1, slot].astype(jnp.float32)

        @pl.when(to == HERE)
        def _():
            final[out] = value
            put(out).start()

        @pl.when(to != HERE)
        def _():
            turned[slot] = value.astype(jnp.bfloat16)

            @pl.when(jnp.logical_not(jnp.logical_and(held_back, i < count - left_out)))
            def _():
                returned(slot, to, out).start()

    def send_late(p):
        @pl.when(role == LATE_NEAR)
        def _():
            to_near(0, p).start()

        @pl.when(late)
        def _():
            to_opp(1, p).start()

    def put(out):
        return pltpu.make_async_copy(final.at[out], out_hbm.at[out], out_sem.at[0])

    put_factor = pltpu.make_async_copy(factors, factor_hbm, table_sem.at[0])

    tables[2].wait()
    tables[3].wait()

    def step(i, carry):
        a, b, wait_a, wait_b, compute, back, relay, relay_at, now, flush, direct, adds, ends_at, slot = decode(pick(i, dos), DO_BASES)

        @pl.when(flush == 1)
        def _():
            for at, code in enumerate(carry):
                settle(i - LAG + at, code)

        carry = tuple(jnp.where(flush == 1, 0, code) for code in carry)

        @pl.when(jnp.logical_and(compute == 0, wait_b == 0))
        def _():
            arrival(b, a).wait_recv()
            relayed(b, a, relay == TO_MATE, relay_at).start()

        @pl.when(wait_a == 1)
        def _():
            arrival_of_look(a).wait_recv()

        @pl.when(jnp.logical_and(wait_b == 1, b >= WHOLE))
        def _():
            arrival_of_look(b).wait_recv()

        @pl.when(jnp.logical_and(wait_b == 1, b < WHOLE))
        def _():
            for p in range(patches):
                arrival(b, p).wait_recv()

                @pl.when(relay != 0)
                def _():
                    relayed(b, p, relay == TO_MATE, relay_at).start()

                if p < patches - 1:

                    @pl.when(adds >= 1)
                    def _():
                        add_patch(w_ref, spec.at[a], spec.at[b], p, acc.at[0])

                    @pl.when(adds == 2)
                    def _():
                        add_patch(w_ref, spec.at[OWN + 1], spec.at[b], p, acc.at[1])

                if p >= patches - 2:

                    @pl.when(jnp.logical_and(now == 1, (role == LATE_NEAR) == (p == patches - 1)))
                    def _():
                        for q in range(patches):
                            send_late(q)

        @pl.when(jnp.logical_and(held_back, i == count - 1))
        def _():
            release()

        @pl.when(compute == 1)
        def _():
            @pl.when(ends_at >= 1)
            def _():
                add_patch(w_ref, spec.at[a], spec.at[b], patches - 1, acc.at[ends_at - 1], cre, cim)

            @pl.when(ends_at == 0)
            def _():
                cross_into(w_ref, spec.at[a], spec.at[b], cre, cim)

            keep, turn = halves(first_ref, second_ref, cre, cim)
            value = keep - turn
            surf[i % HELD] = value
            outbox[slot] = value.astype(jnp.bfloat16)
            value = keep + turn
            surf[HELD + i % HELD] = value
            for by in range(1, nswath):
                outgoing(slot, by).start()

            @pl.when(back == 1)
            def _():
                outbox[slot + 1] = value.astype(jnp.bfloat16)

                @pl.when(direct == 1)
                def _():
                    for by in reversed(range(nswath)):
                        part(slot + 1, by).start()

                @pl.when(direct == 0)
                def _():
                    for by in range(1, nswath):
                        outgoing(slot + 1, by).start()

        @pl.when(i == count - 1)
        def _():
            weigh()

        settle(i - LAG, carry[0])
        return (*carry[1:], pick(i, ends))

    def release():
        pl.semaphore_wait(go, 1)
        for r, leaves in HELD_BACK.items():

            @pl.when(role == r)
            def _():
                slot = 0
                for do, end in step_lists()[r][:-leaves]:
                    if do[4] and end[2] != HERE:
                        returned(slot, jnp.int32(end[2]), end[3]).start()
                    if end[1]:
                        returned(slot + 1, jnp.int32(end[4]), end[5]).start()
                    slot += do[4] + do[5]

    def settle(i, code):
        compute, back, to, out, back_to, back_out, slot = decode(code, END_BASES)

        @pl.when(compute == 1)
        def _():
            at = lax.rem(i + HELD, HELD)

            @pl.when(back == 1)
            def _():
                finish(i, HELD + at, slot + 1, back_to, back_out)

            finish(i, at, slot, to, out)

    def all_heard():
        told = heard.at[pl.ds(1, 4 * nswath - 1)]
        return remote(told, told, heard_send.at[0], heard_recv.at[0], device(-1))

    def weigh():
        all_heard().wait_recv()
        total = []
        for d in range(4):
            for look in range(looks):
                parts = energy[look] if d == 0 else heard[d * nswath, look]
                for by in range(1, nswath):
                    parts = parts + heard[d * nswath + by, look]
                total.append(jnp.sum(parts, axis=(0, 1), keepdims=True))
        scale = BAND * math.sqrt(patches * nswath)

        def factor(look, lag):
            mate = total[look + lag + 1] if lag < 3 else total[3 * looks + look]
            return mask_ref[look, lag].astype(jnp.float32) * scale / jnp.sqrt(total[look] * mate)

        for look in range(looks):
            for lag in range(4):
                factors[look, lag : lag + 1, :] = jnp.broadcast_to(factor(look, lag), (1, WIN))
        put_factor.start()

    def fetch(out):
        @pl.when(bit(backs, out))
        def _():
            remote(turned.at[0], backbox.at[out], back_send.at[0], back_recv.at[out], device(half)).wait_recv()
            final[out] = backbox[out].astype(jnp.float32)
            put(out).start()

    def by_role(counts, act):
        mine_of = pick(role, list(counts))
        for n in sorted(set(counts)):
            if n:

                @pl.when(mine_of == n)
                def _():
                    act(n)

    def drain_units(n):
        sent = spec.at[pl.ds(0, n)]
        remote(sent, sent, unit_send.at[0], spec_recv.at[0], device(-1)).wait_send()

    def drain_boxes(n):
        for by in range(1, nswath):
            sent = inbox.at[by - 1, pl.ds(0, n)]
            remote(sent, sent, box_send.at[by - 1], box_recv.at[by - 1, 0], device(0, by)).wait_send()

    def drain_returns(n):
        sent = turned.at[pl.ds(0, n)]
        remote(sent, sent, back_send.at[0], back_recv.at[0], device(half)).wait_send()

    pending = lax.fori_loop(0, count, step, (jnp.int32(0),) * LAG)
    for at, code in enumerate(pending):
        settle(count - LAG + at, code)
    by_role([looks_sent(r, patches) for r in range(len(RESULTS))], drain_units)

    @pl.when(functools.reduce(jnp.logical_or, [role == at for at in FREES]))
    def _():
        to = jnp.where(odd == 1, me - 1, me + 1)
        pl.semaphore_signal(go, inc=1, device_id=(to, lane), device_id_type=MESH)

    for out in range(OUTS):
        fetch(out)
    place_of = pick(role, [PARTS_OF.get(r, OUTS) for r in range(len(RESULTS))])
    all_parts = remote(parts, parts, parts_send.at[0], parts_recv.at[0], device(half))

    @pl.when(place_of < OUTS)
    def _():
        all_parts.wait_recv()
        value = parts[0].astype(jnp.float32)
        for by in range(1, nswath):
            value = value + parts[by].astype(jnp.float32)
        final[place_of] = value
        put(place_of).start()

    @pl.when(functools.reduce(jnp.logical_or, [role == r for r in PARTS_BY]))
    def _():
        all_parts.wait_send()

    by_role(RESULTS, drain_boxes)
    by_role(RETURNS, drain_returns)
    all_heard().wait_send()
    put_factor.wait()
    pltpu.make_async_copy(final, out_hbm, out_sem.at[0]).wait()


def per_device(images, patch_weight, pair_mask):
    nlook = lax.axis_size("look")
    nswath = lax.axis_size("swath")
    looks, patches = images.shape[:2]
    left, right = forward_tables()
    first, second = inverse_tables()
    rows = WIN // nswath
    hbm = pl.BlockSpec(memory_space=pltpu.HBM)
    smem = pl.BlockSpec(memory_space=pltpu.SMEM)
    dma = pltpu.SemaphoreType.DMA
    unit = (2, BAND, BAND)
    others = max(nswath - 1, 1)
    operands = (patch_weight, pair_mask, images, left, right, first, second)
    surfaces, scales = pl.pallas_call(
        functools.partial(kernel, nlook, nswath),
        in_specs=[smem, smem] + [hbm] * 5,
        out_specs=[pl.BlockSpec(memory_space=pl.ANY)] * 2,
        out_shape=[
            jax.ShapeDtypeStruct((OUTS, rows, WIN), jnp.float32),
            jax.ShapeDtypeStruct((looks, 4, WIN), jnp.float32),
        ],
        scratch_shapes=[
            pltpu.VMEM(left.shape, jnp.bfloat16),
            pltpu.VMEM(right.shape, jnp.bfloat16),
            pltpu.VMEM(first.shape, jnp.bfloat16),
            pltpu.VMEM(second.shape, jnp.bfloat16),
            pltpu.VMEM((looks * patches, 2, PIX, PIX), jnp.bfloat16),
            pltpu.VMEM((BUFFERS, patches) + unit, jnp.bfloat16),
            pltpu.VMEM((looks, 8, 128), jnp.float32),
            pltpu.VMEM((4 * nswath, looks, 8, 128), jnp.float32),
            pltpu.VMEM((BAND, BAND), jnp.bfloat16),
            pltpu.VMEM((BAND, BAND), jnp.bfloat16),
            pltpu.VMEM((2, 2, BAND, BAND), jnp.float32),
            pltpu.VMEM((2 * HELD, WIN, WIN), jnp.float32),
            pltpu.VMEM((SLOTS, WIN, WIN), jnp.bfloat16),
            pltpu.VMEM((others, SLOTS, rows, WIN), jnp.bfloat16),
            pltpu.VMEM((SLOTS, rows, WIN), jnp.bfloat16),
            pltpu.VMEM((OUTS, rows, WIN), jnp.bfloat16),
            pltpu.VMEM((nswath, rows, WIN), jnp.bfloat16),
            pltpu.VMEM((OUTS, rows, WIN), jnp.float32),
            pltpu.VMEM((looks, 4, WIN), jnp.float32),
            dma((2,)),
            dma((AHEAD,)),
            dma((1,)),
            dma(((WHOLE - NEAR) * patches + BUFFERS - WHOLE,)),
            dma((1,)),
            dma((1,)),
            dma((others,)),
            dma((others, SLOTS)),
            dma((1,)),
            dma((OUTS,)),
            dma((1,)),
            dma((1,)),
            dma((1,)),
            pltpu.SemaphoreType.REGULAR,
            pltpu.SemaphoreType.REGULAR,
        ],
        compiler_params=pltpu.CompilerParams(
            collective_id=0, has_side_effects=True, vmem_limit_bytes=52224 << 10
        ),
        name="autofocus",
    )(*[pltpu.with_memory_space_constraint(x, pltpu.HBM) for x in operands])
    return surfaces.reshape(looks, 4, rows, WIN) * scales[:, :, None, :]


def solution(mesh):
    return jax.shard_map(
        per_device,
        mesh=mesh,
        in_specs=(P("look", "swath", None, None, None), P("swath"), P("look", None)),
        out_specs=P("look", None, "swath", None),
        check_vma=False,
    )
```

```python
import functools
import math

import jax
import jax.numpy as jnp
import numpy as np
from jax import lax
from jax.experimental import pallas as pl
from jax.experimental.pallas import tpu as pltpu
from jax.sharding import PartitionSpec as P

PIX = 512
BAND = 256
WIN = 256
HALF = PIX // 2


def phases(rows, cols, row_shift, col_shift):
    phase = (rows[:, None] - row_shift) * (cols[None, :] - col_shift) % PIX
    angle = 2.0 * math.pi / PIX * phase
    return np.cos(angle), np.sin(angle)


def forward_tables():
    left, right = [], []
    for parity in (0, 1):
        re, im = phases(np.arange(parity, BAND, 2), np.arange(HALF), BAND // 2, 0)
        im = -im
        left.append(np.block([[re, -im], [im, re]]))
        right.append(np.block([[re.T, im.T], [-im.T, re.T]]))
    return jnp.asarray(np.stack(left), jnp.bfloat16), jnp.asarray(np.stack(right), jnp.bfloat16)


def inverse_tables():
    order = np.concatenate([np.arange(0, BAND, 2), np.arange(1, BAND, 2)])
    re, im = phases(np.arange(WIN), order, WIN // 2, BAND // 2)
    first = np.concatenate([re, im], axis=0)
    second = np.stack([re.T, im.T])
    return jnp.asarray(first, jnp.bfloat16), jnp.asarray(second, jnp.bfloat16)


def dot(left, right):
    return jnp.dot(left, right, preferred_element_type=jnp.float32)


ROWS = 32
MESH = pl.DeviceIdType.MESH


def spectrum_of(img, left_ref, right_ref):
    re0, re1 = img[0, :HALF, :], img[0, HALF:, :]
    im0, im1 = img[1, :HALF, :], img[1, HALF:, :]
    even = dot(left_ref[0], jnp.concatenate([re0 + re1, im0 + im1], axis=0))
    odd = dot(left_ref[1], jnp.concatenate([re0 - re1, im0 - im1], axis=0))
    quarter = BAND // 2
    parts = []
    for at in (0, quarter):
        parts.append(jnp.concatenate([even[at : at + quarter], odd[at : at + quarter]], axis=0))
    plus = [(part[:, :HALF] + part[:, HALF:]).astype(jnp.bfloat16) for part in parts]
    minus = [(part[:, :HALF] - part[:, HALF:]).astype(jnp.bfloat16) for part in parts]
    spec_even = dot(jnp.concatenate(plus, axis=1), right_ref[0]).astype(jnp.bfloat16)
    spec_odd = dot(jnp.concatenate(minus, axis=1), right_ref[1]).astype(jnp.bfloat16)
    return spec_even, spec_odd


def squares_of(spec_even, spec_odd):
    total = spec_even.astype(jnp.float32) ** 2 + spec_odd.astype(jnp.float32) ** 2
    folded = jnp.sum(total.reshape(BAND // 8, 8, BAND), axis=0)
    return folded[:, : BAND // 2] + folded[:, BAND // 2 :]


def cross_into(w_ref, a_ref, b_ref, cre, cim):
    patches = a_ref.shape[0]

    def step(i, carry):
        rows = pl.ds(pl.multiple_of(i * ROWS, ROWS), ROWS)
        re = jnp.zeros((ROWS, BAND), jnp.float32)
        im = jnp.zeros((ROWS, BAND), jnp.float32)
        for p in range(patches):
            weight = w_ref[p]
            ar = a_ref[p, 0, rows, :].astype(jnp.float32) * weight
            ai = a_ref[p, 1, rows, :].astype(jnp.float32) * weight
            br = b_ref[p, 0, rows, :].astype(jnp.float32)
            bi = b_ref[p, 1, rows, :].astype(jnp.float32)
            re += ar * br + ai * bi
            im += ai * br - ar * bi
        cre[rows, :] = re.astype(jnp.bfloat16)
        cim[rows, :] = im.astype(jnp.bfloat16)
        return carry

    lax.fori_loop(0, BAND // ROWS, step, 0)


def add_patch(w_ref, a_ref, b_ref, p, acc, cre=None, cim=None):
    def step(i, carry):
        rows = pl.ds(pl.multiple_of(i * ROWS, ROWS), ROWS)
        weight = w_ref[p]
        ar = a_ref[p, 0, rows, :].astype(jnp.float32) * weight
        ai = a_ref[p, 1, rows, :].astype(jnp.float32) * weight
        br = b_ref[p, 0, rows, :].astype(jnp.float32)
        bi = b_ref[p, 1, rows, :].astype(jnp.float32)
        re = ar * br + ai * bi
        im = ai * br - ar * bi
        if p:
            re = acc[0, rows, :] + re
            im = acc[1, rows, :] + im
        if cre is None:
            acc[0, rows, :] = re
            acc[1, rows, :] = im
        else:
            cre[rows, :] = re.astype(jnp.bfloat16)
            cim[rows, :] = im.astype(jnp.bfloat16)
        return carry

    lax.fori_loop(0, BAND // ROWS, step, 0)


def halves(first_ref, second_ref, cre, cim):
    from_re = dot(first_ref[...], cre[...]).astype(jnp.bfloat16)
    from_im = dot(first_ref[...], cim[...]).astype(jnp.bfloat16)
    keep = dot(from_re[:WIN], second_ref[0]) - dot(from_re[WIN:], second_ref[1])
    turn = dot(from_im[:WIN], second_ref[1]) + dot(from_im[WIN:], second_ref[0])
    return keep, turn


OWN, NEAR, FAR, LOW, OPP, LAST, HIGH = 0, 2, 4, 5, 5, 8, 11
BUFFERS = 14
WHOLE = LAST
OUTS = 8
HERE, ACROSS, LAST_EVEN, LAST_ODD, ZERO, ONE, HALF_EVEN, HALF_ODD = range(8)
TO_MATE, TO_LAST = 1, 2


def pair_step(a, b, out, to=HERE, wait_a=False, wait_b=False, back=None, relay=(0, 0), compute=True, late=False,
              flush=False, direct=False, adds=0, ends=0):
    back_to, back_out = back if back else (HERE, 0)
    do = (a, b, int(wait_a), int(wait_b), int(compute), int(back is not None), relay[0], relay[1], int(late),
          int(flush), int(direct), adds, ends)
    end = (int(compute), int(back is not None and not direct), to, out, back_to, back_out)
    return do, end


DO_BASES = (16, 16, 2, 2, 2, 2, 4, 16, 2, 2, 2, 4, 4, 32)
END_BASES = (2, 2, 8, 8, 8, 8, 32)


def encode(values, bases):
    code = 0
    for value, base in zip(reversed(values), reversed(bases), strict=True):
        code = code * base + value
    return code


def decode(code, bases):
    values = []
    for base in bases:
        values.append(lax.rem(code, base))
        code = lax.div(code, base)
    return values


def coded(steps):
    codes, slot = [], 0
    for do, end in steps:
        codes.append((encode(do + (slot,), DO_BASES), encode(end + (slot,), END_BASES)))
        slot += do[4] + do[5]
    return codes


def relay_step(b, relay):
    return pair_step(0, b, 0, wait_b=True, relay=relay, compute=False)


def relay_unit(b, p, relay):
    return pair_step(p, b, 0, relay=relay, compute=False)


def opposite(k, direct=False, flush=False):
    out = 4 * k + 3
    return pair_step(OWN + k, OPP + k, out, wait_b=True, back=(ACROSS, out), direct=direct, flush=flush,
                     adds=int(direct), ends=int(direct))


def step_lists():
    first = [pair_step(OWN, OWN + 1, 0)]
    near_pairs = [
        pair_step(OWN, NEAR, 1, wait_b=True),
        pair_step(OWN + 1, NEAR, 4),
        pair_step(OWN, NEAR + 1, 2, wait_b=True),
        pair_step(OWN + 1, NEAR + 1, 5),
    ]
    on_chip = first + near_pairs
    even = on_chip + [pair_step(OWN + 1, FAR, 6, wait_b=True)]
    to_far = (TO_MATE, FAR)

    def odd(end, late=False):
        return (
            first
            + [
                pair_step(OWN, NEAR, 1, wait_b=True, relay=to_far),
                pair_step(OWN + 1, NEAR, 4),
                pair_step(OWN + 1, FAR, 6, wait_b=True),
                pair_step(OWN, NEAR + 1, 2, wait_b=True, late=late),
                pair_step(OWN + 1, NEAR + 1, 5),
            ]
            + end
        )

    def pass_on(p, which):
        at = (NEAR, NEAR + 1, FAR)[which]
        return relay_unit(LOW + which, p, (TO_LAST, at))

    def pass_both(p):
        return [pass_on(p, 0), pass_on(p, 2)]

    hub = (
        pass_both(0)
        + first
        + near_pairs[:2]
        + pass_both(1)
        + near_pairs[2:]
        + pass_both(2)
        + pass_both(3)
        + [
            pair_step(LOW, HIGH, 3, ZERO, wait_b=True, back=(HALF_EVEN, 3)),
            pass_on(0, 1),
            pair_step(LOW + 2, HIGH + 2, 3, ONE, wait_b=True, back=(HALF_ODD, 3)),
            pass_on(1, 1),
            pass_on(2, 1),
            pair_step(LAST, HIGH, 6, LAST_EVEN, wait_a=True),
            pass_on(3, 1),
            pair_step(LAST + 2, HIGH, 4, LAST_ODD, wait_a=True),
            pair_step(LAST + 2, HIGH + 2, 6, LAST_ODD),
            pair_step(LOW + 1, HIGH + 1, 7, ZERO, wait_b=True, back=(HALF_EVEN, 7)),
            pair_step(LAST + 2, HIGH + 1, 5, LAST_ODD),
            pair_step(LAST + 1, HIGH, 1, LAST_ODD, wait_a=True),
            pair_step(LAST + 1, HIGH + 1, 2, LAST_ODD),
            pair_step(OWN + 1, FAR, 6, wait_b=True, flush=True, adds=1, ends=1),
        ]
    )
    hub_odd = first + [
        pair_step(OWN, NEAR + 1, 2, wait_b=True, relay=(TO_MATE, LAST)),
        pair_step(OWN + 1, NEAR + 1, 5),
        pair_step(OWN + 1, FAR, 6, wait_b=True, relay=(TO_MATE, LAST + 1)),
        pair_step(OWN, NEAR, 1, wait_b=True, relay=to_far, adds=3, ends=1),
        pair_step(OWN + 1, NEAR, 4, ends=2),
        pair_step(OWN + 1, OPP + 1, 7, wait_b=True, back=(ACROSS, 7), direct=True, ends=3),
    ]
    last_even = on_chip + [
        opposite(1),
        pair_step(0, FAR, 0, wait_b=True, compute=False, late=True),
        pair_step(OPP + 1, FAR, 6, ACROSS),
    ]
    last_odd = first + [
        relay_step(NEAR, to_far),
        opposite(0),
        pair_step(OPP, NEAR, 1, ACROSS),
        opposite(1),
        pair_step(OPP + 1, NEAR, 4, ACROSS),
        pair_step(OPP + 1, FAR, 6, ACROSS, wait_b=True),
        pair_step(OPP, NEAR + 1, 2, ACROSS, wait_b=True, flush=True),
        pair_step(OPP + 1, NEAR + 1, 5, ACROSS),
    ]
    return (
        even,
        odd([], late=True),
        even,
        odd([opposite(1, True)]),
        hub,
        hub_odd,
        last_even,
        last_odd,
        even,
        odd([opposite(1, True)]),
        even + [opposite(0), opposite(1, True, True)],
        odd([opposite(0)], late=True),
        on_chip + [opposite(0, True)],
        first,
    )


BACK = ((3, 7), (3,), (3,), (3,), (3,), (3,), (6,), (1, 2, 4, 5, 6), (3, 7), (3,), (), (), (6, 7), (1, 2, 3, 4, 5, 6, 7))
PARTS_OF = {1: 7, 2: 7, 4: 7, 6: 3, 11: 7}
PARTS_BY = (3, 5, 9, 10, 12)
HELD_BACK, FREES = {7: (2, 2), 10: (0, 1)}, (6, 11)
SENT = ((), (1,), (0, 1), (0,), (0, 1), (0,), (0,), (), (), (), (), (1,), (1,), (0, 1))
LATE, LATE_NEAR = (1, 11), 6
AHEAD = 2
LAG = 4
HELD = 8
STEPS = max(len(steps) for steps in step_lists())
RESULTS = [sum(end[0] + end[1] for _, end in steps) for steps in step_lists()]
RETURNS = [sum(int(end[2] != HERE) + end[1] for _, end in steps) for steps in step_lists()]
SLOTS = max(sum(do[4] + do[5] for do, _ in steps) for steps in step_lists())


def looks_sent(role, patches):
    relayed = sum((patches if do[3] else 1) for do, _ in step_lists()[role] if do[6])
    return 2 + role % 2 + int(role == 7) + len(SENT[role]) + relayed // patches


def pick(index, values):
    result = jnp.int32(values[0]) if isinstance(values[0], int) else values[0]
    for at, value in enumerate(values[1:], 1):
        result = jnp.where(index == at, value, result)
    return result


def bit(mask, at):
    return lax.rem(lax.div(mask, jnp.int32(2**at)), 2) == 1


def kernel(nlook, nswath, w_ref, mask_ref, img_ref, left_hbm, right_hbm, first_hbm, second_hbm, out_hbm, factor_hbm,
           left_ref, right_ref, first_ref, second_ref, img, spec, energy, heard, cre, cim, acc, surf, outbox, inbox, turned, backbox, parts, final, factors,
           table_sem, img_sem, unit_send, spec_recv,
           heard_send, heard_recv, box_send, box_recv, back_send, back_recv, parts_send, parts_recv, out_sem, ready, go):
    looks, patches = img_ref.shape[:2]
    half = nlook // 2
    hub = half - 4
    me, lane = lax.axis_index("look"), lax.axis_index("swath")
    chip, odd = lax.div(me, 2), lax.rem(me, 2)
    lead = jnp.where(chip == half // 2 - 1, 1, 0)

    def device(look_by, swath_by=0):
        return (lax.rem(me + look_by + nlook, nlook), lax.rem(lane + swath_by, nswath))

    def look_at(u):
        return lax.rem(lead + u // patches, looks)

    def load(u):
        return pltpu.make_async_copy(img_ref.at[look_at(u), u % patches], img.at[u], img_sem.at[u % AHEAD])

    tables = [
        pltpu.make_async_copy(src, dst, table_sem.at[i % 2])
        for i, (src, dst) in enumerate(
            ((left_hbm, left_ref), (right_hbm, right_ref), (first_hbm, first_ref), (second_hbm, second_ref))
        )
    ]
    barrier = pltpu.get_barrier_semaphore()
    behind = []

    def greet(look_bys):
        count = 0
        for look_by in look_bys:
            for by in range(nswath):
                if look_by or by:
                    count += 1
                    to = device(look_by, by)
                    if look_by in (1, 2, half):
                        ends_of_low = jnp.logical_or(to[0] < 2, jnp.logical_and(to[0] >= half - 2, to[0] < half))
                        later = jnp.logical_and(ends_of_low, me >= half)
                        behind.append((later, to))

                        @pl.when(jnp.logical_not(later))
                        def _():
                            pl.semaphore_signal(barrier, inc=1, device_id=to, device_id_type=MESH)
                    else:
                        pl.semaphore_signal(barrier, inc=1, device_id=to, device_id_type=MESH)
        return count

    greeted = greet((half,))
    units = looks * patches
    load(0).start()
    tables[0].start()
    tables[1].start()
    greeted += greet((0, 1, -1, 2, -2))
    met = (0, 1, half - 1, half, half + 1)
    meets = functools.reduce(jnp.logical_or, [me == at for at in met])

    @pl.when(me == hub)
    def _():
        for at in met:
            pl.semaphore_signal(barrier, inc=1, device_id=(jnp.int32(at), lane), device_id_type=MESH)

    @pl.when(meets)
    def _():
        pl.semaphore_signal(barrier, inc=1, device_id=(jnp.int32(hub), lane), device_id_type=MESH)

    expected = jnp.where(me == hub, greeted + len(met), jnp.where(meets, greeted + 1, greeted))
    on_last = chip == half // 2 - 1
    missing = jnp.where(me == 0, 3 * nswath, jnp.where(me == 1, 2 * nswath, jnp.where(on_last, nswath, 0)))

    place = jnp.where(me < half, jnp.int32(1), jnp.int32(5))
    for at, value in ((0, 0), (half // 2 - 2, 2), (half // 2 - 1, 3), (half // 2, 4), (half - 1, 6)):
        place = jnp.where(chip == at, value, place)
    role = 2 * place + odd
    sents = pick(role, [sum(2**at for at in ks) for ks in SENT])
    late = jnp.logical_or(role == LATE[0], jnp.logical_and(role == LATE[1], chip >= half // 2 + 2))
    held_back = functools.reduce(jnp.logical_or, [role == at for at in HELD_BACK])
    held_from, left_out = (
        functools.reduce(lambda n, r: jnp.where(role == r, HELD_BACK[r][at], n), HELD_BACK, 0) for at in (0, 1)
    )

    def remote(src, dst, send, recv, to):
        return pltpu.make_async_remote_copy(
            src_ref=src, dst_ref=dst, send_sem=send, recv_sem=recv, device_id=to, device_id_type=MESH
        )

    def unit(src, at, p, to):
        recv = jnp.where(at < WHOLE, (at - NEAR) * patches + p, (WHOLE - NEAR) * patches + at - WHOLE)
        return remote(spec.at[src, p], spec.at[at, p], unit_send.at[0], spec_recv.at[recv], to)

    def arrival(at, p):
        return unit(at, at, p, device(-1))

    def arrival_of_look(at):
        recv = (WHOLE - NEAR) * patches + at - WHOLE
        return remote(spec.at[at], spec.at[at], unit_send.at[0], spec_recv.at[recv], device(-1))

    def to_near(look, p):
        meeting = jnp.logical_or(me == 0, me == half)
        to = jnp.where(meeting, hub, lax.rem(me - 1 + nlook, nlook))
        at = jnp.where(me == 0, LOW, jnp.where(me == half, HIGH, NEAR)) + look
        return unit(OWN + look, at, p, (to, lane))

    def to_far(look, p):
        meeting = jnp.logical_or(look == 1, jnp.logical_or(me == 1, me == half + 1))
        to = jnp.where(meeting, hub, lax.rem(me - 2 + nlook, nlook))
        at = jnp.where(me == 1, LOW + 2, jnp.where(me == half + 1, HIGH + 2, FAR))
        at = jnp.where(look == 1, LAST + 2, at)
        return unit(OWN + look, at, p, (to, lane))

    def to_opp(look, p):
        return unit(OWN + look, OPP + look, p, device(half))

    def relayed(b, p, mate, at):
        to = jnp.where(mate, lax.rem(me - 1 + nlook, nlook), half - 1)
        return unit(b, at, p, (to, lane))

    def each_send(look, p):
        has_far = jnp.logical_and(odd == 1, jnp.logical_or(look == 0, me == half - 1))
        has_opp = jnp.where(look == 0, bit(sents, 0), bit(sents, 1))

        @pl.when(jnp.logical_and(has_opp, jnp.logical_not(late)))
        def _():
            to_opp(look, p).start()

        held = jnp.logical_and(role == LATE_NEAR, look == 0)

        @pl.when(jnp.logical_not(held))
        def _():
            to_near(look, p).start()

        @pl.when(has_far)
        def _():
            to_far(look, p).start()

    for look in range(looks):
        energy[look] = jnp.zeros((8, 128), jnp.float32)

    def forward(u, carry):
        @pl.when(u == 1)
        def _():
            pl.semaphore_wait(barrier, expected - missing)
            for later, to in behind:

                @pl.when(later)
                def _():
                    pl.semaphore_signal(ready, inc=1, device_id=to, device_id_type=MESH)

        @pl.when(jnp.logical_and(on_last, u == patches + 1))
        def _():
            pl.semaphore_wait(ready, missing)

        @pl.when(u > 0)
        def _():
            each_send(look_at(u - 1), (u - 1) % patches)

        look, p = look_at(u), u % patches
        load(u).wait()

        @pl.when(u == 0)
        def _():
            for first in range(1, AHEAD):
                load(first).start()

        @pl.when(u < units - AHEAD)
        def _():
            load(u + AHEAD).start()

        @pl.when(u == units - AHEAD)
        def _():
            tables[2].start()
            tables[3].start()

        spec_even, spec_odd = spectrum_of(img.at[u], left_ref, right_ref)
        quarter = BAND // 2
        spec[OWN + look, p, 0, :, :quarter] = spec_even[:, :quarter]
        spec[OWN + look, p, 0, :, quarter:] = spec_odd[:, :quarter]
        spec[OWN + look, p, 1, :, :quarter] = spec_even[:, quarter:]
        spec[OWN + look, p, 1, :, quarter:] = spec_odd[:, quarter:]
        energy[look] += w_ref[p] * squares_of(spec_even, spec_odd)
        return carry

    tables[0].wait()
    tables[1].wait()
    lax.fori_loop(0, units, forward, 0)
    each_send(look_at(units - 1), (units - 1) % patches)

    tell = []
    for d, look_by in enumerate((0, 1, 2, half)):
        for by in range(nswath):
            if look_by or by:
                tell.append(remote(energy, heard.at[d * nswath + by], heard_send.at[0], heard_recv.at[0],
                                   device(-look_by, by)))

    @pl.when(me < 2)
    def _():
        pl.semaphore_wait(ready, missing)

    for copy in tell:
        copy.start()

    lists = [coded(steps) for steps in step_lists()]
    count = pick(role, [len(steps) for steps in lists])
    backs = pick(role, [sum(2**at for at in outs) for outs in BACK])
    dos, ends = (
        [pick(role, [steps[i][which] if i < len(steps) else 0 for steps in lists]) for i in range(STEPS)]
        for which in (0, 1)
    )

    rows = WIN // nswath
    mine = pl.ds(pl.multiple_of(lane * rows, rows), rows)

    def outgoing(slot, by):
        at = pl.ds(pl.multiple_of(lax.rem(lane + by, nswath) * rows, rows), rows)
        return remote(outbox.at[slot, at], inbox.at[by - 1, slot], box_send.at[by - 1],
                      box_recv.at[by - 1, slot], device(0, by))

    def part(slot, by):
        at = pl.ds(pl.multiple_of(lax.rem(lane + by, nswath) * rows, rows), rows)
        return remote(outbox.at[slot, at], parts.at[by], parts_send.at[0], parts_recv.at[0], device(half, by))

    def returned(slot, to, out):
        where = pick(to, [me, lax.rem(me + half, nlook), half - 2, half - 1, 0, 1, half, half + 1])
        return remote(turned.at[slot], backbox.at[out], back_send.at[0], back_recv.at[out], (where, lane))

    def finish(i, at, slot, to, out):
        value = surf[at, mine, :]
        for by in range(1, nswath):
            outgoing(slot, by).wait_recv()
            value = value + inbox[by - 1, slot].astype(jnp.float32)

        @pl.when(to == HERE)
        def _():
            final[out] = value
            put(out).start()

        @pl.when(to != HERE)
        def _():
            turned[slot] = value.astype(jnp.bfloat16)

            holds = jnp.logical_and(held_back, jnp.logical_and(i >= held_from, i < count - left_out))

            @pl.when(jnp.logical_not(holds))
            def _():
                returned(slot, to, out).start()

    def send_late(p):
        @pl.when(role == LATE_NEAR)
        def _():
            to_near(0, p).start()

        @pl.when(late)
        def _():
            to_opp(1, p).start()

    def put(out):
        return pltpu.make_async_copy(final.at[out], out_hbm.at[out], out_sem.at[0])

    put_factor = pltpu.make_async_copy(factors, factor_hbm, table_sem.at[0])

    tables[2].wait()
    tables[3].wait()

    def step(i, carry):
        a, b, wait_a, wait_b, compute, back, relay, relay_at, now, flush, direct, adds, ends_at, slot = decode(pick(i, dos), DO_BASES)

        @pl.when(flush == 1)
        def _():
            for at, code in enumerate(carry):
                settle(i - LAG + at, code)

        carry = tuple(jnp.where(flush == 1, 0, code) for code in carry)

        @pl.when(jnp.logical_and(compute == 0, wait_b == 0))
        def _():
            arrival(b, a).wait_recv()
            relayed(b, a, relay == TO_MATE, relay_at).start()

        @pl.when(wait_a == 1)
        def _():
            arrival_of_look(a).wait_recv()

        @pl.when(jnp.logical_and(wait_b == 1, b >= WHOLE))
        def _():
            arrival_of_look(b).wait_recv()

        @pl.when(jnp.logical_and(wait_b == 1, b < WHOLE))
        def _():
            for p in range(patches):

                @pl.when(jnp.logical_or(p == patches - 1, ends_at != 3))
                def _():
                    arrival(b, p).wait_recv()

                @pl.when(relay != 0)
                def _():
                    relayed(b, p, relay == TO_MATE, relay_at).start()

                if p < patches - 1:

                    @pl.when(adds >= 1)
                    def _():
                        add_patch(w_ref, spec.at[a], spec.at[b], p, acc.at[0])

                    @pl.when(adds >= 2)
                    def _():
                        add_patch(w_ref, spec.at[OWN + 1], spec.at[b], p, acc.at[1])

                    @pl.when(adds == 3)
                    def _():
                        arrival(OPP + 1, p).wait_recv()
                        add_patch(w_ref, spec.at[OWN + 1], spec.at[OPP + 1], p, acc.at[2])

                if p >= patches - 2:

                    @pl.when(jnp.logical_and(now == 1, (role == LATE_NEAR) == (p == patches - 1)))
                    def _():
                        for q in range(patches):
                            send_late(q)

        @pl.when(jnp.logical_and(held_back, i == count - 1))
        def _():
            release()

        @pl.when(compute == 1)
        def _():
            @pl.when(ends_at >= 1)
            def _():
                add_patch(w_ref, spec.at[a], spec.at[b], patches - 1, acc.at[ends_at - 1], cre, cim)

            @pl.when(ends_at == 0)
            def _():
                cross_into(w_ref, spec.at[a], spec.at[b], cre, cim)

            keep, turn = halves(first_ref, second_ref, cre, cim)
            value = keep + turn
            surf[HELD + i % HELD] = value

            @pl.when(back == 1)
            def _():
                outbox[slot + 1] = value.astype(jnp.bfloat16)

                @pl.when(direct == 1)
                def _():
                    for by in reversed(range(nswath)):
                        part(slot + 1, by).start()

                @pl.when(direct == 0)
                def _():
                    for by in range(1, nswath):
                        outgoing(slot + 1, by).start()

            value = keep - turn
            surf[i % HELD] = value
            outbox[slot] = value.astype(jnp.bfloat16)
            for by in range(1, nswath):
                outgoing(slot, by).start()

        @pl.when(i == count - 1)
        def _():
            weigh()

        settle(i - LAG, carry[0])
        return (*carry[1:], pick(i, ends))

    def release():
        pl.semaphore_wait(go, 1)
        for r, (begins, leaves) in HELD_BACK.items():

            @pl.when(role == r)
            def _():
                slot = 0
                for at, (do, end) in enumerate(step_lists()[r][:-leaves]):
                    if at >= begins and do[4] and end[2] != HERE:
                        returned(slot, jnp.int32(end[2]), end[3]).start()
                    if at >= begins and end[1]:
                        returned(slot + 1, jnp.int32(end[4]), end[5]).start()
                    slot += do[4] + do[5]

    def settle(i, code):
        compute, back, to, out, back_to, back_out, slot = decode(code, END_BASES)

        @pl.when(compute == 1)
        def _():
            at = lax.rem(i + HELD, HELD)

            @pl.when(back == 1)
            def _():
                finish(i, HELD + at, slot + 1, back_to, back_out)

            finish(i, at, slot, to, out)

    def all_heard():
        told = heard.at[pl.ds(1, 4 * nswath - 1)]
        return remote(told, told, heard_send.at[0], heard_recv.at[0], device(-1))

    def weigh():
        all_heard().wait_recv()
        total = []
        for d in range(4):
            for look in range(looks):
                parts = energy[look] if d == 0 else heard[d * nswath, look]
                for by in range(1, nswath):
                    parts = parts + heard[d * nswath + by, look]
                total.append(jnp.sum(parts, axis=(0, 1), keepdims=True))
        scale = BAND * math.sqrt(patches * nswath)

        def factor(look, lag):
            mate = total[look + lag + 1] if lag < 3 else total[3 * looks + look]
            return mask_ref[look, lag].astype(jnp.float32) * scale / jnp.sqrt(total[look] * mate)

        for look in range(looks):
            for lag in range(4):
                factors[look, lag : lag + 1, :] = jnp.broadcast_to(factor(look, lag), (1, WIN))
        put_factor.start()

    def fetch(out):
        @pl.when(bit(backs, out))
        def _():
            remote(turned.at[0], backbox.at[out], back_send.at[0], back_recv.at[out], device(half)).wait_recv()
            final[out] = backbox[out].astype(jnp.float32)
            put(out).start()

    def by_role(counts, act):
        mine_of = pick(role, list(counts))
        for n in sorted(set(counts)):
            if n:

                @pl.when(mine_of == n)
                def _():
                    act(n)

    def drain_units(n):
        sent = spec.at[pl.ds(0, n)]
        remote(sent, sent, unit_send.at[0], spec_recv.at[0], device(-1)).wait_send()

    def drain_boxes(n):
        for by in range(1, nswath):
            sent = inbox.at[by - 1, pl.ds(0, n)]
            remote(sent, sent, box_send.at[by - 1], box_recv.at[by - 1, 0], device(0, by)).wait_send()

    def drain_returns(n):
        sent = turned.at[pl.ds(0, n)]
        remote(sent, sent, back_send.at[0], back_recv.at[0], device(half)).wait_send()

    pending = lax.fori_loop(0, count, step, (jnp.int32(0),) * LAG)
    for at, code in enumerate(pending):
        settle(count - LAG + at, code)
    by_role([looks_sent(r, patches) for r in range(len(RESULTS))], drain_units)

    @pl.when(functools.reduce(jnp.logical_or, [role == at for at in FREES]))
    def _():
        to = jnp.where(odd == 1, me - 1, me + 1)
        pl.semaphore_signal(go, inc=1, device_id=(to, lane), device_id_type=MESH)

    by_role(RESULTS, drain_boxes)
    by_role(RETURNS, drain_returns)
    all_heard().wait_send()
    put_factor.wait()
    for out in range(OUTS):
        fetch(out)
    place_of = pick(role, [PARTS_OF.get(r, OUTS) for r in range(len(RESULTS))])
    all_parts = remote(parts, parts, parts_send.at[0], parts_recv.at[0], device(half))

    @pl.when(place_of < OUTS)
    def _():
        all_parts.wait_recv()
        value = parts[0].astype(jnp.float32)
        for by in range(1, nswath):
            value = value + parts[by].astype(jnp.float32)
        final[place_of] = value
        put(place_of).start()

    @pl.when(functools.reduce(jnp.logical_or, [role == r for r in PARTS_BY]))
    def _():
        all_parts.wait_send()

    pltpu.make_async_copy(final, out_hbm, out_sem.at[0]).wait()


def per_device(images, patch_weight, pair_mask):
    nlook = lax.axis_size("look")
    nswath = lax.axis_size("swath")
    looks, patches = images.shape[:2]
    left, right = forward_tables()
    first, second = inverse_tables()
    rows = WIN // nswath
    hbm = pl.BlockSpec(memory_space=pltpu.HBM)
    smem = pl.BlockSpec(memory_space=pltpu.SMEM)
    dma = pltpu.SemaphoreType.DMA
    unit = (2, BAND, BAND)
    others = max(nswath - 1, 1)
    operands = (patch_weight, pair_mask, images, left, right, first, second)
    surfaces, scales = pl.pallas_call(
        functools.partial(kernel, nlook, nswath),
        in_specs=[smem, smem] + [hbm] * 5,
        out_specs=[pl.BlockSpec(memory_space=pl.ANY)] * 2,
        out_shape=[
            jax.ShapeDtypeStruct((OUTS, rows, WIN), jnp.float32),
            jax.ShapeDtypeStruct((looks, 4, WIN), jnp.float32),
        ],
        scratch_shapes=[
            pltpu.VMEM(left.shape, jnp.bfloat16),
            pltpu.VMEM(right.shape, jnp.bfloat16),
            pltpu.VMEM(first.shape, jnp.bfloat16),
            pltpu.VMEM(second.shape, jnp.bfloat16),
            pltpu.VMEM((looks * patches, 2, PIX, PIX), jnp.bfloat16),
            pltpu.VMEM((BUFFERS, patches) + unit, jnp.bfloat16),
            pltpu.VMEM((looks, 8, 128), jnp.float32),
            pltpu.VMEM((4 * nswath, looks, 8, 128), jnp.float32),
            pltpu.VMEM((BAND, BAND), jnp.bfloat16),
            pltpu.VMEM((BAND, BAND), jnp.bfloat16),
            pltpu.VMEM((3, 2, BAND, BAND), jnp.float32),
            pltpu.VMEM((2 * HELD, WIN, WIN), jnp.float32),
            pltpu.VMEM((SLOTS, WIN, WIN), jnp.bfloat16),
            pltpu.VMEM((others, SLOTS, rows, WIN), jnp.bfloat16),
            pltpu.VMEM((SLOTS, rows, WIN), jnp.bfloat16),
            pltpu.VMEM((OUTS, rows, WIN), jnp.bfloat16),
            pltpu.VMEM((nswath, rows, WIN), jnp.bfloat16),
            pltpu.VMEM((OUTS, rows, WIN), jnp.float32),
            pltpu.VMEM((looks, 4, WIN), jnp.float32),
            dma((2,)),
            dma((AHEAD,)),
            dma((1,)),
            dma(((WHOLE - NEAR) * patches + BUFFERS - WHOLE,)),
            dma((1,)),
            dma((1,)),
            dma((others,)),
            dma((others, SLOTS)),
            dma((1,)),
            dma((OUTS,)),
            dma((1,)),
            dma((1,)),
            dma((1,)),
            pltpu.SemaphoreType.REGULAR,
            pltpu.SemaphoreType.REGULAR,
        ],
        compiler_params=pltpu.CompilerParams(
            collective_id=0, has_side_effects=True, vmem_limit_bytes=52224 << 10
        ),
        name="autofocus",
    )(*[pltpu.with_memory_space_constraint(x, pltpu.HBM) for x in operands])
    return surfaces.reshape(looks, 4, rows, WIN) * scales[:, :, None, :]


def solution(mesh):
    return jax.shard_map(
        per_device,
        mesh=mesh,
        in_specs=(P("look", "swath", None, None, None), P("swath"), P("look", None)),
        out_specs=P("look", None, "swath", None),
        check_vma=False,
    )
```

```python
import functools
import math

import jax
import jax.numpy as jnp
import numpy as np
from jax import lax
from jax.experimental import pallas as pl
from jax.experimental.pallas import tpu as pltpu
from jax.sharding import PartitionSpec as P

PIX = 512
BAND = 256
WIN = 256
HALF = PIX // 2


def phases(rows, cols, row_shift, col_shift):
    phase = (rows[:, None] - row_shift) * (cols[None, :] - col_shift) % PIX
    angle = 2.0 * math.pi / PIX * phase
    return np.cos(angle), np.sin(angle)


def forward_tables():
    left, right = [], []
    for parity in (0, 1):
        re, im = phases(np.arange(parity, BAND, 2), np.arange(HALF), BAND // 2, 0)
        im = -im
        left.append(np.block([[re, -im], [im, re]]))
        right.append(np.block([[re.T, im.T], [-im.T, re.T]]))
    return jnp.asarray(np.stack(left), jnp.bfloat16), jnp.asarray(np.stack(right), jnp.bfloat16)


def inverse_tables():
    order = np.concatenate([np.arange(0, BAND, 2), np.arange(1, BAND, 2)])
    re, im = phases(np.arange(WIN), order, WIN // 2, BAND // 2)
    first = np.concatenate([re, im], axis=0)
    second = np.stack([re.T, im.T])
    return jnp.asarray(first, jnp.bfloat16), jnp.asarray(second, jnp.bfloat16)


def dot(left, right):
    return jnp.dot(left, right, preferred_element_type=jnp.float32)


ROWS = 32
MESH = pl.DeviceIdType.MESH


def spectrum_of(img, left_ref, right_ref):
    re0, re1 = img[0, :HALF, :], img[0, HALF:, :]
    im0, im1 = img[1, :HALF, :], img[1, HALF:, :]
    even = dot(left_ref[0], jnp.concatenate([re0 + re1, im0 + im1], axis=0))
    odd = dot(left_ref[1], jnp.concatenate([re0 - re1, im0 - im1], axis=0))
    quarter = BAND // 2
    parts = []
    for at in (0, quarter):
        parts.append(jnp.concatenate([even[at : at + quarter], odd[at : at + quarter]], axis=0))
    plus = [(part[:, :HALF] + part[:, HALF:]).astype(jnp.bfloat16) for part in parts]
    minus = [(part[:, :HALF] - part[:, HALF:]).astype(jnp.bfloat16) for part in parts]
    spec_even = dot(jnp.concatenate(plus, axis=1), right_ref[0]).astype(jnp.bfloat16)
    spec_odd = dot(jnp.concatenate(minus, axis=1), right_ref[1]).astype(jnp.bfloat16)
    return spec_even, spec_odd


def squares_of(spec_even, spec_odd):
    total = spec_even.astype(jnp.float32) ** 2 + spec_odd.astype(jnp.float32) ** 2
    folded = jnp.sum(total.reshape(BAND // 8, 8, BAND), axis=0)
    return folded[:, : BAND // 2] + folded[:, BAND // 2 :]


def cross_into(w_ref, a_ref, b_ref, cre, cim):
    patches = a_ref.shape[0]

    def step(i, carry):
        rows = pl.ds(pl.multiple_of(i * ROWS, ROWS), ROWS)
        re = jnp.zeros((ROWS, BAND), jnp.float32)
        im = jnp.zeros((ROWS, BAND), jnp.float32)
        for p in range(patches):
            weight = w_ref[p]
            ar = a_ref[p, 0, rows, :].astype(jnp.float32) * weight
            ai = a_ref[p, 1, rows, :].astype(jnp.float32) * weight
            br = b_ref[p, 0, rows, :].astype(jnp.float32)
            bi = b_ref[p, 1, rows, :].astype(jnp.float32)
            re += ar * br + ai * bi
            im += ai * br - ar * bi
        cre[rows, :] = re.astype(jnp.bfloat16)
        cim[rows, :] = im.astype(jnp.bfloat16)
        return carry

    lax.fori_loop(0, BAND // ROWS, step, 0)


def add_patch(w_ref, a_ref, b_ref, p, acc, cre=None, cim=None):
    def step(i, carry):
        rows = pl.ds(pl.multiple_of(i * ROWS, ROWS), ROWS)
        weight = w_ref[p]
        ar = a_ref[p, 0, rows, :].astype(jnp.float32) * weight
        ai = a_ref[p, 1, rows, :].astype(jnp.float32) * weight
        br = b_ref[p, 0, rows, :].astype(jnp.float32)
        bi = b_ref[p, 1, rows, :].astype(jnp.float32)
        re = ar * br + ai * bi
        im = ai * br - ar * bi
        if p:
            re = acc[0, rows, :] + re
            im = acc[1, rows, :] + im
        if cre is None:
            acc[0, rows, :] = re
            acc[1, rows, :] = im
        else:
            cre[rows, :] = re.astype(jnp.bfloat16)
            cim[rows, :] = im.astype(jnp.bfloat16)
        return carry

    lax.fori_loop(0, BAND // ROWS, step, 0)


def halves(first_ref, second_ref, cre, cim):
    from_re = dot(first_ref[...], cre[...]).astype(jnp.bfloat16)
    from_im = dot(first_ref[...], cim[...]).astype(jnp.bfloat16)
    keep = dot(from_re[:WIN], second_ref[0]) - dot(from_re[WIN:], second_ref[1])
    turn = dot(from_im[:WIN], second_ref[1]) + dot(from_im[WIN:], second_ref[0])
    return keep, turn


OWN, NEAR, FAR, LOW, OPP, LAST, HIGH = 0, 2, 4, 5, 5, 8, 11
BUFFERS = 14
WHOLE = LAST
OUTS = 8
HERE, ACROSS, LAST_EVEN, LAST_ODD, ZERO, ONE, HALF_EVEN, HALF_ODD = range(8)
TO_MATE, TO_LAST = 1, 2


def pair_step(a, b, out, to=HERE, wait_a=False, wait_b=False, back=None, relay=(0, 0), compute=True, late=False,
              flush=False, direct=False, adds=0, ends=0):
    back_to, back_out = back if back else (HERE, 0)
    do = (a, b, int(wait_a), int(wait_b), int(compute), int(back is not None), relay[0], relay[1], int(late),
          int(flush), int(direct), adds, ends)
    end = (int(compute), int(back is not None and not direct), to, out, back_to, back_out)
    return do, end


DO_BASES = (16, 16, 2, 2, 2, 2, 4, 16, 2, 2, 2, 4, 4, 32)
END_BASES = (2, 2, 8, 8, 8, 8, 32)


def encode(values, bases):
    code = 0
    for value, base in zip(reversed(values), reversed(bases), strict=True):
        code = code * base + value
    return code


def decode(code, bases):
    values = []
    for base in bases:
        values.append(lax.rem(code, base))
        code = lax.div(code, base)
    return values


def coded(steps):
    codes, slot = [], 0
    for do, end in steps:
        codes.append((encode(do + (slot,), DO_BASES), encode(end + (slot,), END_BASES)))
        slot += do[4] + do[5]
    return codes


def relay_step(b, relay):
    return pair_step(0, b, 0, wait_b=True, relay=relay, compute=False)


def relay_unit(b, p, relay):
    return pair_step(p, b, 0, relay=relay, compute=False)


def opposite(k, direct=False, flush=False):
    out = 4 * k + 3
    return pair_step(OWN + k, OPP + k, out, wait_b=True, back=(ACROSS, out), direct=direct, flush=flush,
                     adds=int(direct), ends=int(direct))


def step_lists():
    first = [pair_step(OWN, OWN + 1, 0)]
    near_pairs = [
        pair_step(OWN, NEAR, 1, wait_b=True),
        pair_step(OWN + 1, NEAR, 4),
        pair_step(OWN, NEAR + 1, 2, wait_b=True),
        pair_step(OWN + 1, NEAR + 1, 5),
    ]
    on_chip = first + near_pairs
    even = on_chip + [pair_step(OWN + 1, FAR, 6, wait_b=True)]
    to_far = (TO_MATE, FAR)

    def odd(end, late=False):
        return (
            first
            + [
                pair_step(OWN, NEAR, 1, wait_b=True, relay=to_far),
                pair_step(OWN + 1, NEAR, 4),
                pair_step(OWN + 1, FAR, 6, wait_b=True),
                pair_step(OWN, NEAR + 1, 2, wait_b=True, late=late),
                pair_step(OWN + 1, NEAR + 1, 5),
            ]
            + end
        )

    def pass_on(p, which):
        at = (NEAR, NEAR + 1, FAR)[which]
        return relay_unit(LOW + which, p, (TO_LAST, at))

    def pass_both(p):
        return [pass_on(p, 0), pass_on(p, 2)]

    hub = (
        pass_both(0)
        + first
        + near_pairs[:2]
        + pass_both(1)
        + near_pairs[2:]
        + pass_both(2)
        + pass_both(3)
        + [
            pair_step(LOW, HIGH, 3, ZERO, wait_b=True, back=(HALF_EVEN, 3)),
            pass_on(0, 1),
            pair_step(LOW + 2, HIGH + 2, 3, ONE, wait_b=True, back=(HALF_ODD, 3)),
            pass_on(1, 1),
            pass_on(2, 1),
            pair_step(LAST, HIGH, 6, LAST_EVEN, wait_a=True),
            pass_on(3, 1),
            pair_step(LAST + 2, HIGH, 4, LAST_ODD, wait_a=True),
            pair_step(LAST + 2, HIGH + 2, 6, LAST_ODD),
            pair_step(LOW + 1, HIGH + 1, 7, ZERO, wait_b=True, back=(HALF_EVEN, 7)),
            pair_step(LAST + 2, HIGH + 1, 5, LAST_ODD),
            pair_step(LAST + 1, HIGH, 1, LAST_ODD, wait_a=True),
            pair_step(LAST + 1, HIGH + 1, 2, LAST_ODD),
            pair_step(OWN + 1, FAR, 6, wait_b=True, flush=True, adds=1, ends=1),
        ]
    )
    hub_odd = first + [
        pair_step(OWN, NEAR + 1, 2, wait_b=True, relay=(TO_MATE, LAST)),
        pair_step(OWN + 1, NEAR + 1, 5),
        pair_step(OWN + 1, FAR, 6, wait_b=True, relay=(TO_MATE, LAST + 1)),
        pair_step(OWN, NEAR, 1, wait_b=True, relay=to_far, adds=3, ends=1),
        pair_step(OWN + 1, NEAR, 4, ends=2),
        pair_step(OWN + 1, OPP + 1, 7, wait_b=True, back=(ACROSS, 7), direct=True, ends=3),
    ]
    last_even = on_chip + [
        opposite(1),
        pair_step(0, FAR, 0, wait_b=True, compute=False, late=True),
        pair_step(OPP + 1, FAR, 6, ACROSS),
    ]
    last_odd = first + [
        relay_step(NEAR, to_far),
        opposite(0),
        pair_step(OPP, NEAR, 1, ACROSS),
        opposite(1),
        pair_step(OPP + 1, NEAR, 4, ACROSS),
        pair_step(OPP + 1, FAR, 6, ACROSS, wait_b=True),
        pair_step(OPP, NEAR + 1, 2, ACROSS, wait_b=True, flush=True),
        pair_step(OPP + 1, NEAR + 1, 5, ACROSS),
    ]
    return (
        even,
        odd([], late=True),
        even,
        odd([opposite(1, True)]),
        hub,
        hub_odd,
        last_even,
        last_odd,
        even,
        odd([opposite(1, True)]),
        even + [opposite(0), opposite(1, True, True)],
        odd([opposite(0)], late=True),
        on_chip + [opposite(0, True)],
        first,
    )


BACK = ((3, 7), (3,), (3,), (3,), (3,), (3,), (6,), (1, 2, 4, 5, 6), (3, 7), (3,), (), (), (6, 7), (1, 2, 3, 4, 5, 6, 7))
PARTS_OF = {1: 7, 2: 7, 4: 7, 6: 3, 11: 7}
PARTS_BY = (3, 5, 9, 10, 12)
HELD_BACK, FREES = {7: (2, 2), 10: (0, 1)}, (6, 11)
SENT = ((), (1,), (0, 1), (0,), (0, 1), (0,), (0,), (), (), (), (), (1,), (1,), (0, 1))
LATE, LATE_NEAR = (1, 11), 6
AHEAD = 2
LAG = 4
HELD = 8
STEPS = max(len(steps) for steps in step_lists())
RESULTS = [sum(end[0] + end[1] for _, end in steps) for steps in step_lists()]
RETURNS = [sum(int(end[2] != HERE) + end[1] for _, end in steps) for steps in step_lists()]
SLOTS = max(sum(do[4] + do[5] for do, _ in steps) for steps in step_lists())


def looks_sent(role, patches):
    relayed = sum((patches if do[3] else 1) for do, _ in step_lists()[role] if do[6])
    return 2 + role % 2 + int(role == 7) + len(SENT[role]) + relayed // patches


def pick(index, values):
    result = jnp.int32(values[0]) if isinstance(values[0], int) else values[0]
    for at, value in enumerate(values[1:], 1):
        result = jnp.where(index == at, value, result)
    return result


def bit(mask, at):
    return lax.rem(lax.div(mask, jnp.int32(2**at)), 2) == 1


def kernel(nlook, nswath, w_ref, mask_ref, img_ref, left_hbm, right_hbm, first_hbm, second_hbm, out_hbm, factor_hbm,
           left_ref, right_ref, first_ref, second_ref, img, spec, energy, heard, cre, cim, acc, surf, outbox, inbox, turned, backbox, parts, final, factors,
           table_sem, img_sem, unit_send, spec_recv,
           heard_send, heard_recv, box_send, box_recv, back_send, back_recv, parts_send, parts_recv, out_sem, ready, go):
    looks, patches = img_ref.shape[:2]
    half = nlook // 2
    hub = half - 4
    me, lane = lax.axis_index("look"), lax.axis_index("swath")
    chip, odd = lax.div(me, 2), lax.rem(me, 2)
    lead = jnp.where(chip == half // 2 - 1, 1, 0)

    def device(look_by, swath_by=0):
        return (lax.rem(me + look_by + nlook, nlook), lax.rem(lane + swath_by, nswath))

    def look_at(u):
        return lax.rem(lead + u // patches, looks)

    def load(u):
        return pltpu.make_async_copy(img_ref.at[look_at(u), u % patches], img.at[u], img_sem.at[u % AHEAD])

    tables = [
        pltpu.make_async_copy(src, dst, table_sem.at[i % 2])
        for i, (src, dst) in enumerate(
            ((left_hbm, left_ref), (right_hbm, right_ref), (first_hbm, first_ref), (second_hbm, second_ref))
        )
    ]
    barrier = pltpu.get_barrier_semaphore()
    behind = []

    def greet(look_bys):
        count = 0
        for look_by in look_bys:
            for by in range(nswath):
                if look_by or by:
                    count += 1
                    to = device(look_by, by)
                    if look_by:
                        ends_of_low = jnp.logical_or(to[0] < 2, to[0] >= half - 2)
                        if look_by == half and by:
                            ends_of_low = jnp.logical_or(ends_of_low, lax.rem(lax.div(to[0], 2), 2) == 1)
                        later = jnp.logical_and(jnp.logical_and(ends_of_low, to[0] < half), me >= half)
                        behind.append((later, to))

                        @pl.when(jnp.logical_not(later))
                        def _():
                            pl.semaphore_signal(barrier, inc=1, device_id=to, device_id_type=MESH)
                    else:
                        pl.semaphore_signal(barrier, inc=1, device_id=to, device_id_type=MESH)
        return count

    greeted = greet((half,))
    units = looks * patches
    load(0).start()
    tables[0].start()
    tables[1].start()
    greeted += greet((0, 1, -1, 2, -2))
    met = (0, 1, half - 1, half, half + 1)
    meets = functools.reduce(jnp.logical_or, [me == at for at in met])

    @pl.when(me == hub)
    def _():
        for at in met:
            pl.semaphore_signal(barrier, inc=1, device_id=(jnp.int32(at), lane), device_id_type=MESH)

    @pl.when(meets)
    def _():
        pl.semaphore_signal(barrier, inc=1, device_id=(jnp.int32(hub), lane), device_id_type=MESH)

    expected = jnp.where(me == hub, greeted + len(met), jnp.where(meets, greeted + 1, greeted))
    on_last = chip == half // 2 - 1
    missing = jnp.where(jnp.logical_and(me < half, lax.rem(chip, 2) == 1), nswath - 1, 0)
    for at, sources in ((0, 3), (1, 2), (half - 2, 2), (half - 1, 3)):
        missing = jnp.where(me == at, sources * nswath, missing)

    place = jnp.where(me < half, jnp.int32(1), jnp.int32(5))
    for at, value in ((0, 0), (half // 2 - 2, 2), (half // 2 - 1, 3), (half // 2, 4), (half - 1, 6)):
        place = jnp.where(chip == at, value, place)
    role = 2 * place + odd
    sents = pick(role, [sum(2**at for at in ks) for ks in SENT])
    late = jnp.logical_or(role == LATE[0], jnp.logical_and(role == LATE[1], chip >= half // 2 + 2))
    held_back = functools.reduce(jnp.logical_or, [role == at for at in HELD_BACK])
    held_from, left_out = (
        functools.reduce(lambda n, r: jnp.where(role == r, HELD_BACK[r][at], n), HELD_BACK, 0) for at in (0, 1)
    )

    def remote(src, dst, send, recv, to):
        return pltpu.make_async_remote_copy(
            src_ref=src, dst_ref=dst, send_sem=send, recv_sem=recv, device_id=to, device_id_type=MESH
        )

    def unit(src, at, p, to):
        recv = jnp.where(at < WHOLE, (at - NEAR) * patches + p, (WHOLE - NEAR) * patches + at - WHOLE)
        return remote(spec.at[src, p], spec.at[at, p], unit_send.at[0], spec_recv.at[recv], to)

    def arrival(at, p):
        return unit(at, at, p, device(-1))

    def arrival_of_look(at):
        recv = (WHOLE - NEAR) * patches + at - WHOLE
        return remote(spec.at[at], spec.at[at], unit_send.at[0], spec_recv.at[recv], device(-1))

    def to_near(look, p):
        meeting = jnp.logical_or(me == 0, me == half)
        to = jnp.where(meeting, hub, lax.rem(me - 1 + nlook, nlook))
        at = jnp.where(me == 0, LOW, jnp.where(me == half, HIGH, NEAR)) + look
        return unit(OWN + look, at, p, (to, lane))

    def to_far(look, p):
        meeting = jnp.logical_or(look == 1, jnp.logical_or(me == 1, me == half + 1))
        to = jnp.where(meeting, hub, lax.rem(me - 2 + nlook, nlook))
        at = jnp.where(me == 1, LOW + 2, jnp.where(me == half + 1, HIGH + 2, FAR))
        at = jnp.where(look == 1, LAST + 2, at)
        return unit(OWN + look, at, p, (to, lane))

    def to_opp(look, p):
        return unit(OWN + look, OPP + look, p, device(half))

    def relayed(b, p, mate, at):
        to = jnp.where(mate, lax.rem(me - 1 + nlook, nlook), half - 1)
        return unit(b, at, p, (to, lane))

    def each_send(look, p):
        has_far = jnp.logical_and(odd == 1, jnp.logical_or(look == 0, me == half - 1))
        has_opp = jnp.where(look == 0, bit(sents, 0), bit(sents, 1))

        @pl.when(jnp.logical_and(has_opp, jnp.logical_not(late)))
        def _():
            to_opp(look, p).start()

        held = jnp.logical_and(role == LATE_NEAR, look == 0)

        @pl.when(jnp.logical_not(held))
        def _():
            to_near(look, p).start()

        @pl.when(has_far)
        def _():
            to_far(look, p).start()

    for look in range(looks):
        energy[look] = jnp.zeros((8, 128), jnp.float32)

    def forward(u, carry):
        @pl.when(u == 1)
        def _():
            pl.semaphore_wait(barrier, expected - missing)
            for later, to in behind:

                @pl.when(later)
                def _():
                    pl.semaphore_signal(ready, inc=1, device_id=to, device_id_type=MESH)

        @pl.when(jnp.logical_and(on_last, u == patches + 1))
        def _():
            pl.semaphore_wait(ready, missing)

        @pl.when(u > 0)
        def _():
            each_send(look_at(u - 1), (u - 1) % patches)

        look, p = look_at(u), u % patches
        load(u).wait()

        @pl.when(u == 0)
        def _():
            for first in range(1, AHEAD):
                load(first).start()

        @pl.when(u < units - AHEAD)
        def _():
            load(u + AHEAD).start()

        @pl.when(u == units - AHEAD)
        def _():
            tables[2].start()
            tables[3].start()

        spec_even, spec_odd = spectrum_of(img.at[u], left_ref, right_ref)
        quarter = BAND // 2
        spec[OWN + look, p, 0, :, :quarter] = spec_even[:, :quarter]
        spec[OWN + look, p, 0, :, quarter:] = spec_odd[:, :quarter]
        spec[OWN + look, p, 1, :, :quarter] = spec_even[:, quarter:]
        spec[OWN + look, p, 1, :, quarter:] = spec_odd[:, quarter:]
        energy[look] += w_ref[p] * squares_of(spec_even, spec_odd)
        return carry

    tables[0].wait()
    tables[1].wait()
    lax.fori_loop(0, units, forward, 0)
    each_send(look_at(units - 1), (units - 1) % patches)

    tell = []
    for d, look_by in enumerate((0, 1, 2, half)):
        for by in range(nswath):
            if look_by or by:
                tell.append(remote(energy, heard.at[d * nswath + by], heard_send.at[0], heard_recv.at[0],
                                   device(-look_by, by)))

    @pl.when(jnp.logical_and(missing > 0, jnp.logical_not(on_last)))
    def _():
        pl.semaphore_wait(ready, missing)

    for copy in tell:
        copy.start()

    lists = [coded(steps) for steps in step_lists()]
    count = pick(role, [len(steps) for steps in lists])
    backs = pick(role, [sum(2**at for at in outs) for outs in BACK])
    dos, ends = (
        [pick(role, [steps[i][which] if i < len(steps) else 0 for steps in lists]) for i in range(STEPS)]
        for which in (0, 1)
    )

    rows = WIN // nswath
    mine = pl.ds(pl.multiple_of(lane * rows, rows), rows)

    def outgoing(slot, by):
        at = pl.ds(pl.multiple_of(lax.rem(lane + by, nswath) * rows, rows), rows)
        return remote(outbox.at[slot, at], inbox.at[by - 1, slot], box_send.at[by - 1],
                      box_recv.at[by - 1, slot], device(0, by))

    def part(slot, by):
        at = pl.ds(pl.multiple_of(lax.rem(lane + by, nswath) * rows, rows), rows)
        return remote(outbox.at[slot, at], parts.at[by], parts_send.at[0], parts_recv.at[0], device(half, by))

    def returned(slot, to, out):
        where = pick(to, [me, lax.rem(me + half, nlook), half - 2, half - 1, 0, 1, half, half + 1])
        return remote(turned.at[slot], backbox.at[out], back_send.at[0], back_recv.at[out], (where, lane))

    def finish(i, at, slot, to, out):
        value = surf[at, mine, :]
        for by in range(1, nswath):
            outgoing(slot, by).wait_recv()
            value = value + inbox[by - 1, slot].astype(jnp.float32)

        @pl.when(to == HERE)
        def _():
            final[out] = value
            put(out).start()

        @pl.when(to != HERE)
        def _():
            turned[slot] = value.astype(jnp.bfloat16)

            holds = jnp.logical_and(held_back, jnp.logical_and(i >= held_from, i < count - left_out))

            @pl.when(jnp.logical_not(holds))
            def _():
                returned(slot, to, out).start()

    def send_late(p):
        @pl.when(role == LATE_NEAR)
        def _():
            to_near(0, p).start()

        @pl.when(late)
        def _():
            to_opp(1, p).start()

    def put(out):
        return pltpu.make_async_copy(final.at[out], out_hbm.at[out], out_sem.at[0])

    put_factor = pltpu.make_async_copy(factors, factor_hbm, table_sem.at[0])

    tables[2].wait()
    tables[3].wait()

    def step(i, carry):
        a, b, wait_a, wait_b, compute, back, relay, relay_at, now, flush, direct, adds, ends_at, slot = decode(pick(i, dos), DO_BASES)

        @pl.when(flush == 1)
        def _():
            for at, code in enumerate(carry):
                settle(i - LAG + at, code)

        carry = tuple(jnp.where(flush == 1, 0, code) for code in carry)

        @pl.when(jnp.logical_and(compute == 0, wait_b == 0))
        def _():
            arrival(b, a).wait_recv()
            relayed(b, a, relay == TO_MATE, relay_at).start()

        @pl.when(wait_a == 1)
        def _():
            arrival_of_look(a).wait_recv()

        @pl.when(jnp.logical_and(wait_b == 1, b >= WHOLE))
        def _():
            arrival_of_look(b).wait_recv()

        @pl.when(jnp.logical_and(wait_b == 1, b < WHOLE))
        def _():
            for p in range(patches):

                @pl.when(jnp.logical_or(p == patches - 1, ends_at != 3))
                def _():
                    arrival(b, p).wait_recv()

                @pl.when(relay != 0)
                def _():
                    relayed(b, p, relay == TO_MATE, relay_at).start()

                if p < patches - 1:

                    @pl.when(adds >= 1)
                    def _():
                        add_patch(w_ref, spec.at[a], spec.at[b], p, acc.at[0])

                    @pl.when(adds >= 2)
                    def _():
                        add_patch(w_ref, spec.at[OWN + 1], spec.at[b], p, acc.at[1])

                    @pl.when(adds == 3)
                    def _():
                        arrival(OPP + 1, p).wait_recv()
                        add_patch(w_ref, spec.at[OWN + 1], spec.at[OPP + 1], p, acc.at[2])

                if p >= patches - 2:

                    @pl.when(jnp.logical_and(now == 1, (role == LATE_NEAR) == (p == patches - 1)))
                    def _():
                        for q in range(patches):
                            send_late(q)

        @pl.when(jnp.logical_and(held_back, i == count - 1))
        def _():
            release()

        @pl.when(compute == 1)
        def _():
            @pl.when(ends_at >= 1)
            def _():
                add_patch(w_ref, spec.at[a], spec.at[b], patches - 1, acc.at[ends_at - 1], cre, cim)

            @pl.when(ends_at == 0)
            def _():
                cross_into(w_ref, spec.at[a], spec.at[b], cre, cim)

            keep, turn = halves(first_ref, second_ref, cre, cim)
            value = keep + turn
            surf[HELD + i % HELD] = value

            @pl.when(back == 1)
            def _():
                outbox[slot + 1] = value.astype(jnp.bfloat16)

                @pl.when(direct == 1)
                def _():
                    for by in reversed(range(nswath)):
                        part(slot + 1, by).start()

                @pl.when(direct == 0)
                def _():
                    for by in range(1, nswath):
                        outgoing(slot + 1, by).start()

            value = keep - turn
            surf[i % HELD] = value
            outbox[slot] = value.astype(jnp.bfloat16)
            for by in range(1, nswath):
                outgoing(slot, by).start()

        @pl.when(i == count - 1)
        def _():
            weigh()

        settle(i - LAG, carry[0])
        return (*carry[1:], pick(i, ends))

    def release():
        pl.semaphore_wait(go, 1)
        for r, (begins, leaves) in HELD_BACK.items():

            @pl.when(role == r)
            def _():
                slot = 0
                for at, (do, end) in enumerate(step_lists()[r][:-leaves]):
                    if at >= begins and do[4] and end[2] != HERE:
                        returned(slot, jnp.int32(end[2]), end[3]).start()
                    if at >= begins and end[1]:
                        returned(slot + 1, jnp.int32(end[4]), end[5]).start()
                    slot += do[4] + do[5]

    def settle(i, code):
        compute, back, to, out, back_to, back_out, slot = decode(code, END_BASES)

        @pl.when(compute == 1)
        def _():
            at = lax.rem(i + HELD, HELD)

            @pl.when(back == 1)
            def _():
                finish(i, HELD + at, slot + 1, back_to, back_out)

            finish(i, at, slot, to, out)

    def all_heard():
        told = heard.at[pl.ds(1, 4 * nswath - 1)]
        return remote(told, told, heard_send.at[0], heard_recv.at[0], device(-1))

    def weigh():
        all_heard().wait_recv()
        total = []
        for d in range(4):
            for look in range(looks):
                parts = energy[look] if d == 0 else heard[d * nswath, look]
                for by in range(1, nswath):
                    parts = parts + heard[d * nswath + by, look]
                total.append(jnp.sum(parts, axis=(0, 1), keepdims=True))
        scale = BAND * math.sqrt(patches * nswath)

        def factor(look, lag):
            mate = total[look + lag + 1] if lag < 3 else total[3 * looks + look]
            return mask_ref[look, lag].astype(jnp.float32) * scale / jnp.sqrt(total[look] * mate)

        for look in range(looks):
            for lag in range(4):
                factors[look, lag : lag + 1, :] = jnp.broadcast_to(factor(look, lag), (1, WIN))
        put_factor.start()

    def fetch(out):
        @pl.when(bit(backs, out))
        def _():
            remote(turned.at[0], backbox.at[out], back_send.at[0], back_recv.at[out], device(half)).wait_recv()
            final[out] = backbox[out].astype(jnp.float32)
            put(out).start()

    def by_role(counts, act):
        mine_of = pick(role, list(counts))
        for n in sorted(set(counts)):
            if n:

                @pl.when(mine_of == n)
                def _():
                    act(n)

    def drain_units(n):
        sent = spec.at[pl.ds(0, n)]
        remote(sent, sent, unit_send.at[0], spec_recv.at[0], device(-1)).wait_send()

    def drain_boxes(n):
        for by in range(1, nswath):
            sent = inbox.at[by - 1, pl.ds(0, n)]
            remote(sent, sent, box_send.at[by - 1], box_recv.at[by - 1, 0], device(0, by)).wait_send()

    def drain_returns(n):
        sent = turned.at[pl.ds(0, n)]
        remote(sent, sent, back_send.at[0], back_recv.at[0], device(half)).wait_send()

    pending = lax.fori_loop(0, count, step, (jnp.int32(0),) * LAG)
    for at, code in enumerate(pending):
        settle(count - LAG + at, code)
    by_role([looks_sent(r, patches) for r in range(len(RESULTS))], drain_units)

    @pl.when(functools.reduce(jnp.logical_or, [role == at for at in FREES]))
    def _():
        to = jnp.where(odd == 1, me - 1, me + 1)
        pl.semaphore_signal(go, inc=1, device_id=(to, lane), device_id_type=MESH)

    by_role(RESULTS, drain_boxes)
    by_role(RETURNS, drain_returns)
    all_heard().wait_send()
    put_factor.wait()
    for out in range(OUTS):
        fetch(out)
    place_of = pick(role, [PARTS_OF.get(r, OUTS) for r in range(len(RESULTS))])
    all_parts = remote(parts, parts, parts_send.at[0], parts_recv.at[0], device(half))

    @pl.when(place_of < OUTS)
    def _():
        all_parts.wait_recv()
        value = parts[0].astype(jnp.float32)
        for by in range(1, nswath):
            value = value + parts[by].astype(jnp.float32)
        final[place_of] = value
        put(place_of).start()

    @pl.when(functools.reduce(jnp.logical_or, [role == r for r in PARTS_BY]))
    def _():
        all_parts.wait_send()

    pltpu.make_async_copy(final, out_hbm, out_sem.at[0]).wait()


def per_device(images, patch_weight, pair_mask):
    nlook = lax.axis_size("look")
    nswath = lax.axis_size("swath")
    looks, patches = images.shape[:2]
    left, right = forward_tables()
    first, second = inverse_tables()
    rows = WIN // nswath
    hbm = pl.BlockSpec(memory_space=pltpu.HBM)
    smem = pl.BlockSpec(memory_space=pltpu.SMEM)
    dma = pltpu.SemaphoreType.DMA
    unit = (2, BAND, BAND)
    others = max(nswath - 1, 1)
    operands = (patch_weight, pair_mask, images, left, right, first, second)
    surfaces, scales = pl.pallas_call(
        functools.partial(kernel, nlook, nswath),
        in_specs=[smem, smem] + [hbm] * 5,
        out_specs=[pl.BlockSpec(memory_space=pl.ANY)] * 2,
        out_shape=[
            jax.ShapeDtypeStruct((OUTS, rows, WIN), jnp.float32),
            jax.ShapeDtypeStruct((looks, 4, WIN), jnp.float32),
        ],
        scratch_shapes=[
            pltpu.VMEM(left.shape, jnp.bfloat16),
            pltpu.VMEM(right.shape, jnp.bfloat16),
            pltpu.VMEM(first.shape, jnp.bfloat16),
            pltpu.VMEM(second.shape, jnp.bfloat16),
            pltpu.VMEM((looks * patches, 2, PIX, PIX), jnp.bfloat16),
            pltpu.VMEM((BUFFERS, patches) + unit, jnp.bfloat16),
            pltpu.VMEM((looks, 8, 128), jnp.float32),
            pltpu.VMEM((4 * nswath, looks, 8, 128), jnp.float32),
            pltpu.VMEM((BAND, BAND), jnp.bfloat16),
            pltpu.VMEM((BAND, BAND), jnp.bfloat16),
            pltpu.VMEM((3, 2, BAND, BAND), jnp.float32),
            pltpu.VMEM((2 * HELD, WIN, WIN), jnp.float32),
            pltpu.VMEM((SLOTS, WIN, WIN), jnp.bfloat16),
            pltpu.VMEM((others, SLOTS, rows, WIN), jnp.bfloat16),
            pltpu.VMEM((SLOTS, rows, WIN), jnp.bfloat16),
            pltpu.VMEM((OUTS, rows, WIN), jnp.bfloat16),
            pltpu.VMEM((nswath, rows, WIN), jnp.bfloat16),
            pltpu.VMEM((OUTS, rows, WIN), jnp.float32),
            pltpu.VMEM((looks, 4, WIN), jnp.float32),
            dma((2,)),
            dma((AHEAD,)),
            dma((1,)),
            dma(((WHOLE - NEAR) * patches + BUFFERS - WHOLE,)),
            dma((1,)),
            dma((1,)),
            dma((others,)),
            dma((others, SLOTS)),
            dma((1,)),
            dma((OUTS,)),
            dma((1,)),
            dma((1,)),
            dma((1,)),
            pltpu.SemaphoreType.REGULAR,
            pltpu.SemaphoreType.REGULAR,
        ],
        compiler_params=pltpu.CompilerParams(
            collective_id=0, has_side_effects=True, vmem_limit_bytes=52224 << 10
        ),
        name="autofocus",
    )(*[pltpu.with_memory_space_constraint(x, pltpu.HBM) for x in operands])
    return surfaces.reshape(looks, 4, rows, WIN) * scales[:, :, None, :]


def solution(mesh):
    return jax.shard_map(
        per_device,
        mesh=mesh,
        in_specs=(P("look", "swath", None, None, None), P("swath"), P("look", None)),
        out_specs=P("look", None, "swath", None),
        check_vma=False,
    )
```

```python
import functools
import math

import jax
import jax.numpy as jnp
import numpy as np
from jax import lax
from jax.experimental import pallas as pl
from jax.experimental.pallas import tpu as pltpu
from jax.sharding import PartitionSpec as P

PIX = 512
BAND = 256
WIN = 256
HALF = PIX // 2


def phases(rows, cols, row_shift, col_shift):
    phase = (rows[:, None] - row_shift) * (cols[None, :] - col_shift) % PIX
    angle = 2.0 * math.pi / PIX * phase
    return np.cos(angle), np.sin(angle)


def forward_tables():
    left, right = [], []
    for parity in (0, 1):
        re, im = phases(np.arange(parity, BAND, 2), np.arange(HALF), BAND // 2, 0)
        im = -im
        left.append(np.block([[re, -im], [im, re]]))
        right.append(np.block([[re.T, im.T], [-im.T, re.T]]))
    return jnp.asarray(np.stack(left), jnp.bfloat16), jnp.asarray(np.stack(right), jnp.bfloat16)


def inverse_tables():
    order = np.concatenate([np.arange(0, BAND, 2), np.arange(1, BAND, 2)])
    re, im = phases(np.arange(WIN), order, WIN // 2, BAND // 2)
    first = np.concatenate([re, im], axis=0)
    second = np.stack([re.T, im.T])
    return jnp.asarray(first, jnp.bfloat16), jnp.asarray(second, jnp.bfloat16)


def dot(left, right):
    return jnp.dot(left, right, preferred_element_type=jnp.float32)


ROWS = 32
MESH = pl.DeviceIdType.MESH


def spectrum_of(img, left_ref, right_ref):
    re0, re1 = img[0, :HALF, :], img[0, HALF:, :]
    im0, im1 = img[1, :HALF, :], img[1, HALF:, :]
    even = dot(left_ref[0], jnp.concatenate([re0 + re1, im0 + im1], axis=0))
    odd = dot(left_ref[1], jnp.concatenate([re0 - re1, im0 - im1], axis=0))
    quarter = BAND // 2
    parts = []
    for at in (0, quarter):
        parts.append(jnp.concatenate([even[at : at + quarter], odd[at : at + quarter]], axis=0))
    plus = [(part[:, :HALF] + part[:, HALF:]).astype(jnp.bfloat16) for part in parts]
    minus = [(part[:, :HALF] - part[:, HALF:]).astype(jnp.bfloat16) for part in parts]
    spec_even = dot(jnp.concatenate(plus, axis=1), right_ref[0]).astype(jnp.bfloat16)
    spec_odd = dot(jnp.concatenate(minus, axis=1), right_ref[1]).astype(jnp.bfloat16)
    return spec_even, spec_odd


def squares_of(spec_even, spec_odd):
    total = spec_even.astype(jnp.float32) ** 2 + spec_odd.astype(jnp.float32) ** 2
    folded = jnp.sum(total.reshape(BAND // 8, 8, BAND), axis=0)
    return folded[:, : BAND // 2] + folded[:, BAND // 2 :]


def cross_into(w_ref, a_ref, b_ref, cre, cim):
    patches = a_ref.shape[0]

    def step(i, carry):
        rows = pl.ds(pl.multiple_of(i * ROWS, ROWS), ROWS)
        re = jnp.zeros((ROWS, BAND), jnp.float32)
        im = jnp.zeros((ROWS, BAND), jnp.float32)
        for p in range(patches):
            weight = w_ref[p]
            ar = a_ref[p, 0, rows, :].astype(jnp.float32) * weight
            ai = a_ref[p, 1, rows, :].astype(jnp.float32) * weight
            br = b_ref[p, 0, rows, :].astype(jnp.float32)
            bi = b_ref[p, 1, rows, :].astype(jnp.float32)
            re += ar * br + ai * bi
            im += ai * br - ar * bi
        cre[rows, :] = re.astype(jnp.bfloat16)
        cim[rows, :] = im.astype(jnp.bfloat16)
        return carry

    lax.fori_loop(0, BAND // ROWS, step, 0)


def add_patch(w_ref, a_ref, b_ref, p, acc, cre=None, cim=None):
    def step(i, carry):
        rows = pl.ds(pl.multiple_of(i * ROWS, ROWS), ROWS)
        weight = w_ref[p]
        ar = a_ref[p, 0, rows, :].astype(jnp.float32) * weight
        ai = a_ref[p, 1, rows, :].astype(jnp.float32) * weight
        br = b_ref[p, 0, rows, :].astype(jnp.float32)
        bi = b_ref[p, 1, rows, :].astype(jnp.float32)
        re = ar * br + ai * bi
        im = ai * br - ar * bi
        if p:
            re = acc[0, rows, :] + re
            im = acc[1, rows, :] + im
        if cre is None:
            acc[0, rows, :] = re
            acc[1, rows, :] = im
        else:
            cre[rows, :] = re.astype(jnp.bfloat16)
            cim[rows, :] = im.astype(jnp.bfloat16)
        return carry

    lax.fori_loop(0, BAND // ROWS, step, 0)


def halves(first_ref, second_ref, cre, cim):
    from_re = dot(first_ref[...], cre[...]).astype(jnp.bfloat16)
    from_im = dot(first_ref[...], cim[...]).astype(jnp.bfloat16)
    keep = dot(from_re[:WIN], second_ref[0]) - dot(from_re[WIN:], second_ref[1])
    turn = dot(from_im[:WIN], second_ref[1]) + dot(from_im[WIN:], second_ref[0])
    return keep, turn


OWN, NEAR, FAR, LOW, OPP, LAST, HIGH = 0, 2, 4, 5, 5, 8, 11
BUFFERS = 14
WHOLE = LAST
OUTS = 8
HERE, ACROSS, LAST_EVEN, LAST_ODD, ZERO, ONE, HALF_EVEN, HALF_ODD = range(8)
TO_MATE, TO_LAST = 1, 2


def pair_step(a, b, out, to=HERE, wait_a=False, wait_b=False, back=None, relay=(0, 0), compute=True, late=False,
              flush=False, direct=False, adds=0, ends=0):
    back_to, back_out = back if back else (HERE, 0)
    do = (a, b, int(wait_a), int(wait_b), int(compute), int(back is not None), relay[0], relay[1], int(late),
          int(flush), int(direct), adds, ends)
    end = (int(compute), int(back is not None and not direct), to, out, back_to, back_out)
    return do, end


DO_BASES = (16, 16, 2, 2, 2, 2, 4, 16, 2, 2, 2, 4, 4, 32)
END_BASES = (2, 2, 8, 8, 8, 8, 32)


def encode(values, bases):
    code = 0
    for value, base in zip(reversed(values), reversed(bases), strict=True):
        code = code * base + value
    return code


def decode(code, bases):
    values = []
    for base in bases:
        values.append(lax.rem(code, base))
        code = lax.div(code, base)
    return values


def coded(steps):
    codes, slot = [], 0
    for do, end in steps:
        codes.append((encode(do + (slot,), DO_BASES), encode(end + (slot,), END_BASES)))
        slot += do[4] + do[5]
    return codes


def relay_step(b, relay):
    return pair_step(0, b, 0, wait_b=True, relay=relay, compute=False)


def relay_unit(b, p, relay):
    return pair_step(p, b, 0, relay=relay, compute=False)


def opposite(k, direct=False, flush=False):
    out = 4 * k + 3
    return pair_step(OWN + k, OPP + k, out, wait_b=True, back=(ACROSS, out), direct=direct, flush=flush,
                     adds=int(direct), ends=int(direct))


def step_lists():
    first = [pair_step(OWN, OWN + 1, 0)]
    near_pairs = [
        pair_step(OWN, NEAR, 1, wait_b=True),
        pair_step(OWN + 1, NEAR, 4),
        pair_step(OWN, NEAR + 1, 2, wait_b=True),
        pair_step(OWN + 1, NEAR + 1, 5),
    ]
    on_chip = first + near_pairs
    even = on_chip + [pair_step(OWN + 1, FAR, 6, wait_b=True)]
    to_far = (TO_MATE, FAR)

    def odd(end, late=False):
        return (
            first
            + [
                pair_step(OWN, NEAR, 1, wait_b=True, relay=to_far),
                pair_step(OWN + 1, NEAR, 4),
                pair_step(OWN + 1, FAR, 6, wait_b=True),
                pair_step(OWN, NEAR + 1, 2, wait_b=True, late=late),
                pair_step(OWN + 1, NEAR + 1, 5),
            ]
            + end
        )

    def pass_on(p, which):
        at = (NEAR, NEAR + 1, FAR)[which]
        return relay_unit(LOW + which, p, (TO_LAST, at))

    def pass_both(p):
        return [pass_on(p, 0), pass_on(p, 2)]

    hub = (
        pass_both(0)
        + first
        + near_pairs[:2]
        + pass_both(1)
        + near_pairs[2:]
        + pass_both(2)
        + pass_both(3)
        + [
            pair_step(LOW, HIGH, 3, ZERO, wait_b=True, back=(HALF_EVEN, 3)),
            pass_on(0, 1),
            pair_step(LOW + 2, HIGH + 2, 3, ONE, wait_b=True, back=(HALF_ODD, 3)),
            pass_on(1, 1),
            pass_on(2, 1),
            pair_step(LAST, HIGH, 6, LAST_EVEN, wait_a=True),
            pass_on(3, 1),
            pair_step(LAST + 2, HIGH, 4, LAST_ODD, wait_a=True),
            pair_step(LAST + 2, HIGH + 2, 6, LAST_ODD),
            pair_step(LOW + 1, HIGH + 1, 7, ZERO, wait_b=True, back=(HALF_EVEN, 7)),
            pair_step(LAST + 2, HIGH + 1, 5, LAST_ODD),
            pair_step(LAST + 1, HIGH, 1, LAST_ODD, wait_a=True),
            pair_step(LAST + 1, HIGH + 1, 2, LAST_ODD),
            pair_step(OWN + 1, FAR, 6, wait_b=True, flush=True, adds=1, ends=1),
        ]
    )
    hub_odd = first + [
        pair_step(OWN, NEAR + 1, 2, wait_b=True, relay=(TO_MATE, LAST)),
        pair_step(OWN + 1, NEAR + 1, 5),
        pair_step(OWN + 1, FAR, 6, wait_b=True, relay=(TO_MATE, LAST + 1)),
        pair_step(OWN, NEAR, 1, wait_b=True, relay=to_far, adds=3, ends=1),
        pair_step(OWN + 1, NEAR, 4, ends=2),
        pair_step(OWN + 1, OPP + 1, 7, wait_b=True, back=(ACROSS, 7), direct=True, ends=3),
    ]
    last_even = on_chip + [
        opposite(1),
        pair_step(0, FAR, 0, wait_b=True, compute=False, late=True),
        pair_step(OPP + 1, FAR, 6, ACROSS),
    ]
    last_odd = first + [
        relay_step(NEAR, to_far),
        opposite(0),
        pair_step(OPP, NEAR, 1, ACROSS),
        opposite(1),
        pair_step(OPP + 1, NEAR, 4, ACROSS),
        pair_step(OPP + 1, FAR, 6, ACROSS, wait_b=True),
        pair_step(OPP, NEAR + 1, 2, ACROSS, wait_b=True, flush=True),
        pair_step(OPP + 1, NEAR + 1, 5, ACROSS),
    ]
    return (
        even,
        odd([], late=True),
        even,
        odd([opposite(1, True)]),
        hub,
        hub_odd,
        last_even,
        last_odd,
        even,
        odd([opposite(1, True)]),
        even + [opposite(0), opposite(1, True, True)],
        odd([opposite(0)], late=True),
        on_chip + [opposite(0, True)],
        first,
    )


BACK = ((3, 7), (3,), (3,), (3,), (3,), (3,), (6,), (1, 2, 4, 5, 6), (3, 7), (3,), (), (), (6, 7), (1, 2, 3, 4, 5, 6, 7))
PARTS_OF = {1: 7, 2: 7, 4: 7, 6: 3, 11: 7}
PARTS_BY = (3, 5, 9, 10, 12)
HELD_BACK, FREES = {7: (2, 2), 10: (0, 1)}, (6, 11)
SENT = ((), (1,), (0, 1), (0,), (0, 1), (0,), (0,), (), (), (), (), (1,), (1,), (0, 1))
LATE, LATE_NEAR = (1, 11), 6
AHEAD = 2
LAG = 4
HELD = 8
STEPS = max(len(steps) for steps in step_lists())
RESULTS = [sum(end[0] + end[1] for _, end in steps) for steps in step_lists()]
RETURNS = [sum(int(end[2] != HERE) + end[1] for _, end in steps) for steps in step_lists()]
SLOTS = max(sum(do[4] + do[5] for do, _ in steps) for steps in step_lists())


def looks_sent(role, patches):
    relayed = sum((patches if do[3] else 1) for do, _ in step_lists()[role] if do[6])
    return 2 + role % 2 + int(role == 7) + len(SENT[role]) + relayed // patches


def pick(index, values):
    result = jnp.int32(values[0]) if isinstance(values[0], int) else values[0]
    for at, value in enumerate(values[1:], 1):
        result = jnp.where(index == at, value, result)
    return result


def bit(mask, at):
    return lax.rem(lax.div(mask, jnp.int32(2**at)), 2) == 1


def kernel(nlook, nswath, w_ref, mask_ref, img_ref, left_hbm, right_hbm, first_hbm, second_hbm, out_hbm, factor_hbm,
           left_ref, right_ref, first_ref, second_ref, img, spec, energy, heard, cre, cim, acc, surf, outbox, inbox, turned, backbox, parts, final, factors,
           table_sem, img_sem, unit_send, spec_recv,
           heard_send, heard_recv, box_send, box_recv, back_send, back_recv, parts_send, parts_recv, out_sem, ready, go):
    looks, patches = img_ref.shape[:2]
    half = nlook // 2
    hub = half - 4
    me, lane = lax.axis_index("look"), lax.axis_index("swath")
    chip, odd = lax.div(me, 2), lax.rem(me, 2)
    lead = jnp.where(chip == half // 2 - 1, 1, 0)

    def device(look_by, swath_by=0):
        return (lax.rem(me + look_by + nlook, nlook), lax.rem(lane + swath_by, nswath))

    def look_at(u):
        return lax.rem(lead + u // patches, looks)

    def load(u):
        return pltpu.make_async_copy(img_ref.at[look_at(u), u % patches], img.at[u], img_sem.at[u % AHEAD])

    tables = [
        pltpu.make_async_copy(src, dst, table_sem.at[i % 2])
        for i, (src, dst) in enumerate(
            ((left_hbm, left_ref), (right_hbm, right_ref), (first_hbm, first_ref), (second_hbm, second_ref))
        )
    ]
    barrier = pltpu.get_barrier_semaphore()
    behind = []

    def greet(look_bys):
        count = 0
        for look_by in look_bys:
            for by in range(nswath):
                if look_by or by:
                    count += 1
                    to = device(look_by, by)
                    if look_by:
                        ends_of_low = jnp.logical_or(to[0] < 2, to[0] >= half - 2)
                        if look_by == half and by:
                            ends_of_low = jnp.logical_or(ends_of_low, lax.rem(lax.div(to[0], 2), 2) == 1)
                        later = jnp.logical_and(jnp.logical_and(ends_of_low, to[0] < half), me >= half)
                        behind.append((later, to))

                        @pl.when(jnp.logical_not(later))
                        def _():
                            pl.semaphore_signal(barrier, inc=1, device_id=to, device_id_type=MESH)
                    else:
                        pl.semaphore_signal(barrier, inc=1, device_id=to, device_id_type=MESH)
        return count

    greeted = greet((half,))
    units = looks * patches
    load(0).start()
    tables[0].start()
    tables[1].start()
    greeted += greet((0, 1, -1, 2, -2))
    met = (0, 1, half - 1, half, half + 1)
    meets = functools.reduce(jnp.logical_or, [me == at for at in met])

    @pl.when(me == hub)
    def _():
        for at in met:
            pl.semaphore_signal(barrier, inc=1, device_id=(jnp.int32(at), lane), device_id_type=MESH)

    @pl.when(meets)
    def _():
        pl.semaphore_signal(barrier, inc=1, device_id=(jnp.int32(hub), lane), device_id_type=MESH)

    expected = jnp.where(me == hub, greeted + len(met), jnp.where(meets, greeted + 1, greeted))
    on_last = chip == half // 2 - 1
    missing = jnp.where(jnp.logical_and(me < half, lax.rem(chip, 2) == 1), nswath - 1, 0)
    for at, sources in ((0, 3), (1, 2), (half - 2, 2), (half - 1, 3)):
        missing = jnp.where(me == at, sources * nswath, missing)

    place = jnp.where(me < half, jnp.int32(1), jnp.int32(5))
    for at, value in ((0, 0), (half // 2 - 2, 2), (half // 2 - 1, 3), (half // 2, 4), (half - 1, 6)):
        place = jnp.where(chip == at, value, place)
    role = 2 * place + odd
    sents = pick(role, [sum(2**at for at in ks) for ks in SENT])
    late = jnp.logical_or(role == LATE[0], jnp.logical_and(role == LATE[1], chip >= half // 2 + 2))
    held_back = functools.reduce(jnp.logical_or, [role == at for at in HELD_BACK])
    held_from, left_out = (
        functools.reduce(lambda n, r: jnp.where(role == r, HELD_BACK[r][at], n), HELD_BACK, 0) for at in (0, 1)
    )

    def remote(src, dst, send, recv, to):
        return pltpu.make_async_remote_copy(
            src_ref=src, dst_ref=dst, send_sem=send, recv_sem=recv, device_id=to, device_id_type=MESH
        )

    def unit(src, at, p, to):
        recv = jnp.where(at < WHOLE, (at - NEAR) * patches + p, (WHOLE - NEAR) * patches + at - WHOLE)
        return remote(spec.at[src, p], spec.at[at, p], unit_send.at[0], spec_recv.at[recv], to)

    def arrival(at, p):
        return unit(at, at, p, device(-1))

    def arrival_of_look(at):
        recv = (WHOLE - NEAR) * patches + at - WHOLE
        return remote(spec.at[at], spec.at[at], unit_send.at[0], spec_recv.at[recv], device(-1))

    def to_near(look, p):
        meeting = jnp.logical_or(me == 0, me == half)
        to = jnp.where(meeting, hub, lax.rem(me - 1 + nlook, nlook))
        at = jnp.where(me == 0, LOW, jnp.where(me == half, HIGH, NEAR)) + look
        return unit(OWN + look, at, p, (to, lane))

    def to_far(look, p):
        meeting = jnp.logical_or(look == 1, jnp.logical_or(me == 1, me == half + 1))
        to = jnp.where(meeting, hub, lax.rem(me - 2 + nlook, nlook))
        at = jnp.where(me == 1, LOW + 2, jnp.where(me == half + 1, HIGH + 2, FAR))
        at = jnp.where(look == 1, LAST + 2, at)
        return unit(OWN + look, at, p, (to, lane))

    def to_opp(look, p):
        return unit(OWN + look, OPP + look, p, device(half))

    def relayed(b, p, mate, at):
        to = jnp.where(mate, lax.rem(me - 1 + nlook, nlook), half - 1)
        return unit(b, at, p, (to, lane))

    def each_send(look, p):
        has_far = jnp.logical_and(odd == 1, jnp.logical_or(look == 0, me == half - 1))
        has_opp = jnp.where(look == 0, bit(sents, 0), bit(sents, 1))

        @pl.when(jnp.logical_and(has_opp, jnp.logical_not(late)))
        def _():
            to_opp(look, p).start()

        held = jnp.logical_and(role == LATE_NEAR, look == 0)

        @pl.when(jnp.logical_not(held))
        def _():
            to_near(look, p).start()

        @pl.when(has_far)
        def _():
            to_far(look, p).start()

    for look in range(looks):
        energy[look] = jnp.zeros((8, 128), jnp.float32)

    def forward(u, carry):
        @pl.when(u == 1)
        def _():
            pl.semaphore_wait(barrier, expected - missing)
            for later, to in behind:

                @pl.when(later)
                def _():
                    pl.semaphore_signal(ready, inc=1, device_id=to, device_id_type=MESH)

        @pl.when(jnp.logical_and(on_last, u == patches + 1))
        def _():
            pl.semaphore_wait(ready, missing)

        @pl.when(u > 0)
        def _():
            each_send(look_at(u - 1), (u - 1) % patches)

        look, p = look_at(u), u % patches
        load(u).wait()

        @pl.when(u == 0)
        def _():
            for first in range(1, AHEAD):
                load(first).start()

        @pl.when(u < units - AHEAD)
        def _():
            load(u + AHEAD).start()

        @pl.when(u == units - AHEAD)
        def _():
            tables[2].start()
            tables[3].start()

        spec_even, spec_odd = spectrum_of(img.at[u], left_ref, right_ref)
        quarter = BAND // 2
        spec[OWN + look, p, 0, :, :quarter] = spec_even[:, :quarter]
        spec[OWN + look, p, 0, :, quarter:] = spec_odd[:, :quarter]
        spec[OWN + look, p, 1, :, :quarter] = spec_even[:, quarter:]
        spec[OWN + look, p, 1, :, quarter:] = spec_odd[:, quarter:]
        energy[look] += w_ref[p] * squares_of(spec_even, spec_odd)
        return carry

    tables[0].wait()
    tables[1].wait()
    lax.fori_loop(0, units, forward, 0)
    each_send(look_at(units - 1), (units - 1) % patches)

    tell = []
    for d, look_by in enumerate((0, 1, 2, half)):
        for by in range(nswath):
            if look_by or by:
                tell.append(remote(energy, heard.at[d * nswath + by], heard_send.at[0], heard_recv.at[0],
                                   device(-look_by, by)))

    @pl.when(jnp.logical_and(missing > 0, jnp.logical_not(on_last)))
    def _():
        pl.semaphore_wait(ready, missing)

    for copy in tell:
        copy.start()

    lists = [coded(steps) for steps in step_lists()]
    count = pick(role, [len(steps) for steps in lists])
    backs = pick(role, [sum(2**at for at in outs) for outs in BACK])
    dos, ends = (
        [pick(role, [steps[i][which] if i < len(steps) else 0 for steps in lists]) for i in range(STEPS)]
        for which in (0, 1)
    )

    rows = WIN // nswath
    mine = pl.ds(pl.multiple_of(lane * rows, rows), rows)

    def outgoing(slot, by):
        at = pl.ds(pl.multiple_of(lax.rem(lane + by, nswath) * rows, rows), rows)
        return remote(outbox.at[slot, at], inbox.at[by - 1, slot], box_send.at[by - 1],
                      box_recv.at[by - 1, slot], device(0, by))

    def part(slot, by):
        at = pl.ds(pl.multiple_of(lax.rem(lane + by, nswath) * rows, rows), rows)
        return remote(outbox.at[slot, at], parts.at[by], parts_send.at[0], parts_recv.at[0], device(half, by))

    def returned(slot, to, out):
        where = pick(to, [me, lax.rem(me + half, nlook), half - 2, half - 1, 0, 1, half, half + 1])
        return remote(turned.at[slot], backbox.at[out], back_send.at[0], back_recv.at[out], (where, lane))

    def finish(i, at, slot, to, out):
        value = surf[at, mine, :]
        for by in range(1, nswath):
            outgoing(slot, by).wait_recv()
            value = value + inbox[by - 1, slot].astype(jnp.float32)

        @pl.when(to == HERE)
        def _():
            final[out] = value
            put(out).start()

        @pl.when(to != HERE)
        def _():
            turned[slot] = value.astype(jnp.bfloat16)

            holds = jnp.logical_and(held_back, jnp.logical_and(i >= held_from, i < count - left_out))

            @pl.when(jnp.logical_not(holds))
            def _():
                returned(slot, to, out).start()

    def send_late(p):
        @pl.when(role == LATE_NEAR)
        def _():
            to_near(0, p).start()

        @pl.when(late)
        def _():
            to_opp(1, p).start()

    def put(out):
        return pltpu.make_async_copy(final.at[out], out_hbm.at[out], out_sem.at[0])

    put_factor = pltpu.make_async_copy(factors, factor_hbm, table_sem.at[0])

    tables[2].wait()
    tables[3].wait()

    def step(i, carry):
        a, b, wait_a, wait_b, compute, back, relay, relay_at, now, flush, direct, adds, ends_at, slot = decode(pick(i, dos), DO_BASES)

        @pl.when(flush == 1)
        def _():
            for at, code in enumerate(carry):
                settle(i - LAG + at, code)

        carry = tuple(jnp.where(flush == 1, 0, code) for code in carry)

        @pl.when(jnp.logical_and(compute == 0, wait_b == 0))
        def _():
            arrival(b, a).wait_recv()
            relayed(b, a, relay == TO_MATE, relay_at).start()

        @pl.when(wait_a == 1)
        def _():
            arrival_of_look(a).wait_recv()

        @pl.when(jnp.logical_and(wait_b == 1, b >= WHOLE))
        def _():
            arrival_of_look(b).wait_recv()

        @pl.when(jnp.logical_and(wait_b == 1, b < WHOLE))
        def _():
            for p in range(patches):

                @pl.when(jnp.logical_or(p == patches - 1, ends_at != 3))
                def _():
                    arrival(b, p).wait_recv()

                @pl.when(relay != 0)
                def _():
                    relayed(b, p, relay == TO_MATE, relay_at).start()

                if p < patches - 1:

                    @pl.when(adds >= 1)
                    def _():
                        add_patch(w_ref, spec.at[a], spec.at[b], p, acc.at[0])

                    @pl.when(adds >= 2)
                    def _():
                        add_patch(w_ref, spec.at[OWN + 1], spec.at[b], p, acc.at[1])

                    @pl.when(adds == 3)
                    def _():
                        arrival(OPP + 1, p).wait_recv()
                        add_patch(w_ref, spec.at[OWN + 1], spec.at[OPP + 1], p, acc.at[2])

                if p >= patches - 2:

                    @pl.when(jnp.logical_and(now == 1, p == patches - 2))
                    def _():
                        for q in range(patches):
                            send_late(q)

        @pl.when(jnp.logical_and(held_back, i == count - 1))
        def _():
            release()

        @pl.when(compute == 1)
        def _():
            @pl.when(ends_at >= 1)
            def _():
                add_patch(w_ref, spec.at[a], spec.at[b], patches - 1, acc.at[ends_at - 1], cre, cim)

            @pl.when(ends_at == 0)
            def _():
                cross_into(w_ref, spec.at[a], spec.at[b], cre, cim)

            keep, turn = halves(first_ref, second_ref, cre, cim)
            value = keep + turn
            surf[HELD + i % HELD] = value

            @pl.when(back == 1)
            def _():
                outbox[slot + 1] = value.astype(jnp.bfloat16)

                @pl.when(direct == 1)
                def _():
                    for by in reversed(range(nswath)):
                        part(slot + 1, by).start()

                @pl.when(direct == 0)
                def _():
                    for by in range(1, nswath):
                        outgoing(slot + 1, by).start()

            value = keep - turn
            surf[i % HELD] = value
            outbox[slot] = value.astype(jnp.bfloat16)
            for by in range(1, nswath):
                outgoing(slot, by).start()

        @pl.when(i == count - 1)
        def _():
            weigh()

        settle(i - LAG, carry[0])
        return (*carry[1:], pick(i, ends))

    def release():
        pl.semaphore_wait(go, 1)
        for r, (begins, leaves) in HELD_BACK.items():

            @pl.when(role == r)
            def _():
                slot = 0
                for at, (do, end) in enumerate(step_lists()[r][:-leaves]):
                    if at >= begins and do[4] and end[2] != HERE:
                        returned(slot, jnp.int32(end[2]), end[3]).start()
                    if at >= begins and end[1]:
                        returned(slot + 1, jnp.int32(end[4]), end[5]).start()
                    slot += do[4] + do[5]

    def settle(i, code):
        compute, back, to, out, back_to, back_out, slot = decode(code, END_BASES)

        @pl.when(compute == 1)
        def _():
            at = lax.rem(i + HELD, HELD)

            @pl.when(back == 1)
            def _():
                finish(i, HELD + at, slot + 1, back_to, back_out)

            finish(i, at, slot, to, out)

    def all_heard():
        told = heard.at[pl.ds(1, 4 * nswath - 1)]
        return remote(told, told, heard_send.at[0], heard_recv.at[0], device(-1))

    def weigh():
        all_heard().wait_recv()
        total = []
        for d in range(4):
            for look in range(looks):
                parts = energy[look] if d == 0 else heard[d * nswath, look]
                for by in range(1, nswath):
                    parts = parts + heard[d * nswath + by, look]
                total.append(jnp.sum(parts, axis=(0, 1), keepdims=True))
        scale = BAND * math.sqrt(patches * nswath)

        def factor(look, lag):
            mate = total[look + lag + 1] if lag < 3 else total[3 * looks + look]
            return mask_ref[look, lag].astype(jnp.float32) * scale / jnp.sqrt(total[look] * mate)

        for look in range(looks):
            for lag in range(4):
                factors[look, lag : lag + 1, :] = jnp.broadcast_to(factor(look, lag), (1, WIN))
        put_factor.start()

    def fetch(out):
        @pl.when(bit(backs, out))
        def _():
            remote(turned.at[0], backbox.at[out], back_send.at[0], back_recv.at[out], device(half)).wait_recv()
            final[out] = backbox[out].astype(jnp.float32)
            put(out).start()

    def by_role(counts, act):
        mine_of = pick(role, list(counts))
        for n in sorted(set(counts)):
            if n:

                @pl.when(mine_of == n)
                def _():
                    act(n)

    def drain_units(n):
        sent = spec.at[pl.ds(0, n)]
        remote(sent, sent, unit_send.at[0], spec_recv.at[0], device(-1)).wait_send()

    def drain_boxes(n):
        for by in range(1, nswath):
            sent = inbox.at[by - 1, pl.ds(0, n)]
            remote(sent, sent, box_send.at[by - 1], box_recv.at[by - 1, 0], device(0, by)).wait_send()

    def drain_returns(n):
        sent = turned.at[pl.ds(0, n)]
        remote(sent, sent, back_send.at[0], back_recv.at[0], device(half)).wait_send()

    pending = lax.fori_loop(0, count, step, (jnp.int32(0),) * LAG)
    for at, code in enumerate(pending):
        settle(count - LAG + at, code)
    by_role([looks_sent(r, patches) for r in range(len(RESULTS))], drain_units)

    @pl.when(functools.reduce(jnp.logical_or, [role == at for at in FREES]))
    def _():
        to = jnp.where(odd == 1, me - 1, me + 1)
        pl.semaphore_signal(go, inc=1, device_id=(to, lane), device_id_type=MESH)

    by_role(RESULTS, drain_boxes)
    by_role(RETURNS, drain_returns)
    all_heard().wait_send()
    put_factor.wait()
    for out in range(OUTS):
        fetch(out)
    place_of = pick(role, [PARTS_OF.get(r, OUTS) for r in range(len(RESULTS))])
    all_parts = remote(parts, parts, parts_send.at[0], parts_recv.at[0], device(half))

    @pl.when(place_of < OUTS)
    def _():
        all_parts.wait_recv()
        value = parts[0].astype(jnp.float32)
        for by in range(1, nswath):
            value = value + parts[by].astype(jnp.float32)
        final[place_of] = value
        put(place_of).start()

    @pl.when(functools.reduce(jnp.logical_or, [role == r for r in PARTS_BY]))
    def _():
        all_parts.wait_send()

    pltpu.make_async_copy(final, out_hbm, out_sem.at[0]).wait()


def per_device(images, patch_weight, pair_mask):
    nlook = lax.axis_size("look")
    nswath = lax.axis_size("swath")
    looks, patches = images.shape[:2]
    left, right = forward_tables()
    first, second = inverse_tables()
    rows = WIN // nswath
    hbm = pl.BlockSpec(memory_space=pltpu.HBM)
    smem = pl.BlockSpec(memory_space=pltpu.SMEM)
    dma = pltpu.SemaphoreType.DMA
    unit = (2, BAND, BAND)
    others = max(nswath - 1, 1)
    operands = (patch_weight, pair_mask, images, left, right, first, second)
    surfaces, scales = pl.pallas_call(
        functools.partial(kernel, nlook, nswath),
        in_specs=[smem, smem] + [hbm] * 5,
        out_specs=[pl.BlockSpec(memory_space=pl.ANY)] * 2,
        out_shape=[
            jax.ShapeDtypeStruct((OUTS, rows, WIN), jnp.float32),
            jax.ShapeDtypeStruct((looks, 4, WIN), jnp.float32),
        ],
        scratch_shapes=[
            pltpu.VMEM(left.shape, jnp.bfloat16),
            pltpu.VMEM(right.shape, jnp.bfloat16),
            pltpu.VMEM(first.shape, jnp.bfloat16),
            pltpu.VMEM(second.shape, jnp.bfloat16),
            pltpu.VMEM((looks * patches, 2, PIX, PIX), jnp.bfloat16),
            pltpu.VMEM((BUFFERS, patches) + unit, jnp.bfloat16),
            pltpu.VMEM((looks, 8, 128), jnp.float32),
            pltpu.VMEM((4 * nswath, looks, 8, 128), jnp.float32),
            pltpu.VMEM((BAND, BAND), jnp.bfloat16),
            pltpu.VMEM((BAND, BAND), jnp.bfloat16),
            pltpu.VMEM((3, 2, BAND, BAND), jnp.float32),
            pltpu.VMEM((2 * HELD, WIN, WIN), jnp.float32),
            pltpu.VMEM((SLOTS, WIN, WIN), jnp.bfloat16),
            pltpu.VMEM((others, SLOTS, rows, WIN), jnp.bfloat16),
            pltpu.VMEM((SLOTS, rows, WIN), jnp.bfloat16),
            pltpu.VMEM((OUTS, rows, WIN), jnp.bfloat16),
            pltpu.VMEM((nswath, rows, WIN), jnp.bfloat16),
            pltpu.VMEM((OUTS, rows, WIN), jnp.float32),
            pltpu.VMEM((looks, 4, WIN), jnp.float32),
            dma((2,)),
            dma((AHEAD,)),
            dma((1,)),
            dma(((WHOLE - NEAR) * patches + BUFFERS - WHOLE,)),
            dma((1,)),
            dma((1,)),
            dma((others,)),
            dma((others, SLOTS)),
            dma((1,)),
            dma((OUTS,)),
            dma((1,)),
            dma((1,)),
            dma((1,)),
            pltpu.SemaphoreType.REGULAR,
            pltpu.SemaphoreType.REGULAR,
        ],
        compiler_params=pltpu.CompilerParams(
            collective_id=0, has_side_effects=True, vmem_limit_bytes=52224 << 10
        ),
        name="autofocus",
    )(*[pltpu.with_memory_space_constraint(x, pltpu.HBM) for x in operands])
    return surfaces.reshape(looks, 4, rows, WIN) * scales[:, :, None, :]


def solution(mesh):
    return jax.shard_map(
        per_device,
        mesh=mesh,
        in_specs=(P("look", "swath", None, None, None), P("swath"), P("look", None)),
        out_specs=P("look", None, "swath", None),
        check_vma=False,
    )
```
